256 devices in a mesh: movie: 128 (over z, y, x), user: 2 (over core).
Axes of the slice: x: 4, y: 4, z: 8, core: 2. Of those that a mesh axis runs over, the one named last changes fastest.
Arguments:
- movie_ids: int32 [1024, 128], P(('movie', 'user')), may hold values from 0 to 17919, as said below
- ratings: int32 [1024, 128], P(('movie', 'user')), may hold values from 0 to 4
- valid: int32 [1024, 128], P(('movie', 'user')), may hold values from 0 to 1, as said below
- weights: bfloat16 [5, 17920, 1024], P(None, 'movie'), may hold values from -0.5 to 0.5
- vis_bias: float32 [5, 17920], P(None, 'movie'), may hold values from -5 to 260
- hid_bias: float32 [1024], replicated, may hold values from -5 to 5
Outputs:
- weight_grad: float32 [5, 17920, 1024], P(None, 'movie')
- visible_grad: float32 [5, 17920], P(None, 'movie')
- hidden_grad: float32 [1024], replicated
- positive_hidden: float32 [1024, 1024], P(('movie', 'user'))
The draws below stay inside these ranges and needn't reach their ends.
Inputs may be any that keep to these rules, and one draw needn't show every extreme that they name: `movie_ids`: movie ids within one user's block are distinct. Of the slots with valid 1 among the users of one device (4 consecutive users), at most 12 name movies of any one block of 140 consecutive movie ids; in every draw some such block takes exactly 12 from the users of every device. Slots with valid 0 are padding and count nowhere.
All inputs are finite; a program needn't handle non-finite values.
Results may differ from the reference program's by a relative error of at most 0.0054.
Values may be sent and summed in bfloat16 or wider, within the bound.
A program may use at most 64 MiB of HBM per device.

```python
import math
import jax
import jax.numpy as jnp
from jax import lax

F = 1024
LEVELS = 5
MOVIES = 17920
SLOTS = 128
USR_DEV = 4
OWNERS = 128
MOV_DEV = 140
USERS = 1024
CAP = 12


def rating_layout(key):
    base_key = jax.random.fold_in(key, 7101)
    busiest = jax.random.randint(jax.random.fold_in(base_key, 1), (), 0, OWNERS)
    device_slots = USR_DEV * SLOTS
    position = jnp.arange(device_slots, dtype=jnp.int32)
    listed = jnp.where(position < CAP, busiest, (busiest + 1 + (position - CAP) % (OWNERS - 1)) % OWNERS)
    devices = USERS // USR_DEV
    device_keys = jax.random.split(jax.random.fold_in(base_key, 2), devices)
    shuffle = jax.vmap(lambda single: jax.random.permutation(single, device_slots))(device_keys)
    owner_ids = listed[shuffle].reshape(USERS, SLOTS).astype(jnp.int32)
    offsets_table = jax.random.randint(jax.random.fold_in(base_key, 3), (USERS, OWNERS), 0, MOV_DEV)
    matching = owner_ids[:, :, None] == owner_ids[:, None, :]
    slot_index = jnp.arange(SLOTS, dtype=jnp.int32)
    earlier = slot_index[None, :] < slot_index[:, None]
    occurrence = jnp.sum((matching & earlier[None]).astype(jnp.int32), axis=2)
    offset = jnp.take_along_axis(offsets_table, owner_ids, axis=1)
    local_index = (offset + occurrence) % MOV_DEV
    movie_block = (owner_ids * MOV_DEV + local_index).astype(jnp.int32)
    coin_flip = jax.random.randint(jax.random.fold_in(base_key, 4), (USERS, SLOTS), 0, 4)
    usable = jnp.where(owner_ids == busiest, 1, jnp.where(coin_flip > 0, 1, 0)).astype(jnp.int32)
    return (movie_block, usable)


def draw_movie_ids(key, part):
    return rating_layout(key)[0]


def draw_valid(key, part):
    return rating_layout(key)[1]


def draw_vis_bias(key, part):
    baseline = jnp.clip(jax.random.normal(jax.random.fold_in(key, 11), (LEVELS, MOVIES), jnp.float32), -4.0, 4.0)
    return baseline.astype(jnp.float32)


def plant(result, own_key, least, top_value):
    longest = result.shape.index(max(result.shape))
    spots = []
    for shift in (0, 1):
        where = [jax.random.randint(jax.random.fold_in(own_key, axis), (), 0, length) for axis, length in enumerate(result.shape)]
        where[longest] = (where[longest] + shift) % result.shape[longest]
        spots.append(tuple(where))
    return result.at[spots[0]].set(least).at[spots[1]].set(top_value)


def block_scale(key, extent, pieces, smallest, high):
    def one(axis_at, parts):
        steps = jax.random.uniform(jax.random.fold_in(jax.random.fold_in(key, 6), axis_at), (parts,), jnp.float32, smallest / len(pieces), high / len(pieces))
        return jnp.repeat(jnp.exp(steps), extent[axis_at] // parts).reshape((-1,) + (1,) * (len(extent) - axis_at - 1))

    level = one(*pieces[0])
    for cut in pieces[1:]:
        level = level * one(*cut)
    return level


def normal_values(stream_key, shape, scale, most, cuts=(), kind=jnp.bfloat16):
    drawn = scale * jax.random.normal(stream_key, shape, jnp.float32)
    if cuts:
        drawn = drawn * block_scale(stream_key, shape, cuts, -0.22, 0.18)
    return jnp.clip(drawn, -most, most).astype(kind)


def setup_inputs(seed: int = 0) -> dict:
    streams_of = jax.random.split(jax.random.key(seed), 7)
    movie_ids = draw_movie_ids(jax.random.fold_in(streams_of[6], 71), 0)
    ratings = plant(jax.random.randint(streams_of[1], (USERS, SLOTS), 0, LEVELS), jax.random.fold_in(streams_of[1], 1), 0, LEVELS - 1).astype(jnp.int32)
    valid = draw_valid(jax.random.fold_in(streams_of[6], 71), 0)
    weights = normal_values(streams_of[3], (LEVELS, MOVIES, F), SLOTS ** -0.5, 0.5, ((1, 128),))
    vis_bias = draw_vis_bias(jax.random.fold_in(streams_of[6], 71), 0)
    hid_bias = normal_values(streams_of[5], (F,), 1.0, 5.0, (), jnp.float32)
    return {"movie_ids": movie_ids, "ratings": ratings, "valid": valid, "weights": weights, "vis_bias": vis_bias, "hid_bias": hid_bias}


def reference(movie_ids, ratings, valid, weights, vis_bias, hid_bias):
    user_count, slot_count = movie_ids.shape
    levels, movies, hidden = weights.shape
    block_size = math.gcd(user_count, 16)
    block_count = user_count // block_size
    rating_levels = jnp.arange(levels, dtype=jnp.int32)
    highest_rating = lax.Precision.HIGHEST

    def advance(totals, block_index):
        weight_grad, visible_grad, hidden_grad = totals
        first_row = (block_index * block_size).astype(jnp.int32)
        movie_block = lax.dynamic_slice_in_dim(movie_ids, first_row, block_size, 0)
        rating_block = lax.dynamic_slice_in_dim(ratings, first_row, block_size, 0)
        usable = lax.dynamic_slice_in_dim(valid, first_row, block_size, 0).astype(jnp.float32)
        movie_weight_rows = weights[:, movie_block].astype(jnp.float32)
        visible_bias_rows = vis_bias[:, movie_block]
        observed_mask = (rating_block[None] == rating_levels[:, None, None]).astype(jnp.float32) * usable[None]
        positive_statistics = jnp.einsum("drp,drpv->rv", observed_mask, movie_weight_rows, precision=highest_rating)
        hidden_pos = jax.nn.sigmoid(hid_bias[None, :] + positive_statistics)
        positive_lower_part = lax.optimization_barrier(hidden_pos.astype(jnp.bfloat16)).astype(jnp.float32)
        rating_logits = visible_bias_rows + jnp.einsum("cm,rcjm->rcj", positive_lower_part, movie_weight_rows, precision=highest_rating)
        largest = jnp.max(rating_logits, axis=0, keepdims=True)
        exponent = jnp.exp(rating_logits - largest)
        softened = (exponent / jnp.sum(exponent, axis=0, keepdims=True)).astype(jnp.bfloat16)
        reconstructed_ratings = lax.optimization_barrier(softened).astype(jnp.float32) * usable[None]
        negative_statistics = jnp.einsum("drp,drpv->rv", reconstructed_ratings, movie_weight_rows, precision=highest_rating)
        hidden_neg = jax.nn.sigmoid(hid_bias[None, :] + negative_statistics)
        negative_low = lax.optimization_barrier(hidden_neg.astype(jnp.bfloat16)).astype(jnp.float32)
        contrib = observed_mask[..., None] * positive_lower_part[None, :, None, :] - reconstructed_ratings[..., None] * negative_low[None, :, None, :]
        weight_grad = weight_grad.at[:, movie_block].add(contrib)
        visible_grad = visible_grad.at[:, movie_block].add(observed_mask - reconstructed_ratings)
        hidden_grad = hidden_grad + jnp.sum(hidden_pos - hidden_neg, axis=0)
        return (weight_grad, visible_grad, hidden_grad), hidden_pos

    initial = (jnp.zeros((levels, movies, hidden), jnp.float32), jnp.zeros((levels, movies), jnp.float32), jnp.zeros((hidden,), jnp.float32))
    totals, hidden_rows = lax.scan(advance, initial, jnp.arange(block_count, dtype=jnp.int32))
    weight_grad, visible_grad, hidden_grad = totals
    return weight_grad, visible_grad, hidden_grad, hidden_rows.reshape(user_count, hidden)
```

```python
import functools

import jax
import jax.numpy as jnp
from jax import lax
from jax.experimental import pallas as pl
from jax.experimental.pallas import tpu as pltpu
from jax.sharding import Mesh
from jax.sharding import PartitionSpec as P

LEVELS = 5
MOV = 140
PAD = 144
COLS = LEVELS * PAD
F = 1024
NZ, NXY = 8, 16
CAP = 12
USERS = 512
GROUPS = 2
U = USERS // GROUPS
R = U // NXY
ALL = ("z", "y", "x", "core")
MESH = pl.DeviceIdType.MESH
F32, BF16 = jnp.float32, jnp.bfloat16


def dot(a, b, ca, cb):
    return lax.dot_general(a, b, (((ca,), (cb,)), ((), ())), preferred_element_type=F32)


def kernel(
    ids_ref, rat_ref, val_ref, w_ref, vb_ref, hb_ref,
    wg_ref, vg_ref, hg_ref, ph_ref,
    w_sc, vb_pad, vbc, t2d, t_send, d1, d2, s_sc, r_sc, l_sc,
    p_sc, r1, q_sc, r2, hid, pos_own, acc_sc, own_sc, oth_sc,
    hz, hxy, hco, vco,
    dz_s, dz_r, dx_s, dx_r, cz_s, cz_r, cx_s, cx_r, hz_s, hz_r, hx_s, hx_r, co_s, co_r,
):
    z, y, x, core = [lax.axis_index(a) for a in ALL]
    xy = y * 4 + x
    other = (z, y, x, 1 - core)

    def xy_peer(d):
        return lax.rem(y + d // 4, 4), lax.rem(x + lax.rem(d, 4), 4)

    def z_peer(d):
        return lax.rem(z + d, NZ)

    def xy_copies(src, dst, send, recv):
        def copy(d):
            ty, tx = xy_peer(d)
            return pltpu.make_async_remote_copy(
                src(ty * 4 + tx), dst(d), send.at[d], recv.at[d],
                device_id=(z, ty, tx, core), device_id_type=MESH,
            )

        return NXY, copy

    def z_copies(src, dst, send, recv):
        def copy(d):
            tz = z_peer(d)
            return pltpu.make_async_remote_copy(
                src(tz), dst(d), send.at[d], recv.at[d],
                device_id=(tz, y, x, core), device_id_type=MESH,
            )

        return NZ, copy

    def each(copies, act):
        n, copy = copies

        def step(d, carry):
            act(copy(d))
            return carry

        lax.fori_loop(1, n, step, 0)

    def start(copies):
        each(copies, lambda c: c.start())

    def arrived(copies):
        each(copies, lambda c: c.wait_recv())

    def sent(copies):
        each(copies, lambda c: c.wait_send())

    barrier = pltpu.get_barrier_semaphore()

    def greet_xy(d, carry):
        ty, tx = xy_peer(d)
        pl.semaphore_signal(barrier, 1, device_id=(z, ty, tx, core), device_id_type=MESH)
        return carry

    def greet_z(d, carry):
        pl.semaphore_signal(barrier, 1, device_id=(z_peer(d), y, x, core), device_id_type=MESH)
        return carry

    lax.fori_loop(1, NZ, greet_z, 0)
    lax.fori_loop(1, NXY, greet_xy, 0)
    pl.semaphore_signal(barrier, 1, device_id=other, device_id_type=MESH)

    ids = ids_ref[...]
    owner = jnp.floor((ids.astype(F32) + 0.5) * (1.0 / MOV)).astype(jnp.int32)
    column = rat_ref[...] * PAD + (ids - owner * MOV) + 1
    high = lax.shift_right_logical(column, 5).astype(F32)
    low = (column & 31).astype(F32)
    owner = jnp.where(val_ref[...] == 1, owner, -1)
    row = lax.broadcasted_iota(jnp.int32, (128, 128), 0)
    lane = lax.broadcasted_iota(jnp.int32, (128, 128), 1)
    before = jnp.where(row < lane, 1.0, 0.0).astype(BF16)
    rank_row = (row & 15).astype(F32)
    user_row = lax.shift_right_logical(row, 4) & 3
    table = jnp.zeros((128, 128), F32)
    for u in range(4):
        hot = jnp.where(owner[u : u + 1] == row, 1.0, 0.0)
        hot_low = hot.astype(BF16)
        rank = jnp.sum(hot * dot(hot_low, before, 1, 0), axis=0, keepdims=True)
        part = jnp.where(row < 64, high[u : u + 1], low[u : u + 1])
        pick = jnp.where((user_row == u) & (rank_row == rank), part, 0.0)
        table = table + dot(hot_low, pick.astype(BF16), 1, 1)
    t2d[...] = table

    def spread(i, carry):
        t_send[i // NXY, lax.rem(i, NXY)] = t2d[pl.ds(i, 1), :]
        return carry

    lax.fori_loop(0, 128, spread, 0)

    for k in range(LEVELS):
        w_sc[k * PAD + 128 : (k + 1) * PAD] = jnp.zeros((PAD - 128, F), BF16)
        w_sc[k * PAD : k * PAD + MOV] = w_ref[k]
    vb_pad[...] = jnp.zeros((8, 256), F32)
    vb_pad[0:LEVELS, 0:MOV] = vb_ref[...]
    bias_columns = jnp.transpose(vb_pad[...])
    for k in range(LEVELS):
        vbc[k * PAD : (k + 1) * PAD] = jnp.broadcast_to(bias_columns[0:PAD, k : k + 1], (PAD, 128))

    pl.semaphore_wait(barrier, NZ - 1 + NXY - 1 + 1)

    to_z = z_copies(lambda t: t_send.at[t], lambda d: d1.at[z], dz_s, dz_r)
    start(to_z)
    d1[z] = t_send[z]
    arrived(to_z)
    to_xy = xy_copies(lambda t: d1.at[:, t], lambda d: d2.at[xy], dx_s, dx_r)
    start(to_xy)
    d2[xy] = d1[:, xy]
    arrived(to_xy)
    sent(to_z)
    sent(to_xy)

    def collect(i, carry):
        t2d[pl.ds(i, 1), :] = d2[i // NZ, lax.rem(i, NZ)]
        return carry

    lax.fori_loop(0, 128, collect, 0)
    got = jnp.transpose(t2d[...])
    chosen = got[0:64] * 32.0 + got[64:128] - 1.0

    def group_rows(c, g, t):
        return hid.at[c, pl.ds(pl.multiple_of(g * U + t * R, R), R), :]

    def rs_xy(c, g):
        return xy_copies(
            lambda t: p_sc.at[c, pl.ds(pl.multiple_of(g * U + t * R, R), R), :],
            lambda d: r1.at[c, g, d], cx_s.at[2 * c, g], cx_r.at[2 * c, g],
        )

    def rs_z(c, g):
        return z_copies(
            lambda t: q_sc.at[c, g, t], lambda d: r2.at[c, g, d], cz_s.at[2 * c, g], cz_r.at[2 * c, g]
        )

    def own_piece(c, g):
        rows = pl.ds(pl.multiple_of(g * U + xy * R, R), R)
        return hid.at[c, rows, pl.ds(pl.multiple_of(z * 128, 128), 128)]

    def ag_z(c, g):
        return z_copies(
            lambda t: own_piece(c, g), lambda d: own_piece(c, g), cz_s.at[2 * c + 1, g], cz_r.at[2 * c + 1, g]
        )

    def ag_xy(c, g):
        return xy_copies(
            lambda t: group_rows(c, g, xy), lambda d: group_rows(c, g, xy),
            cx_s.at[2 * c + 1, g], cx_r.at[2 * c + 1, g],
        )

    def partial_inputs(c, g, visible):
        p_sc[c, g * U : (g + 1) * U] = dot(visible, w_sc[...], 0, 0).astype(BF16)
        start(rs_xy(c, g))

    def plane_sum(c, g):
        arrived(rs_xy(c, g))
        rows = pl.ds(pl.multiple_of(g * U + xy * R, R), R)
        for f in range(NZ):
            cut = slice(f * 128, (f + 1) * 128)
            total = p_sc[c, rows, cut].astype(F32)
            for d in range(1, NXY):
                total = total + r1[c, g, d, :, cut].astype(F32)
            q_sc[c, g, f] = total.astype(BF16)
        start(rs_z(c, g))

    def ring_sum(c, g):
        arrived(rs_z(c, g))
        total = q_sc[c, g, z].astype(F32)
        for d in range(1, NZ):
            total = total + r2[c, g, d].astype(F32)
        value = 1.0 / (1.0 + jnp.exp(-(total + hb_ref[z])))
        own_piece(c, g)[...] = value.astype(BF16)
        start(ag_z(c, g))
        return value

    def ring_gather(c, g):
        arrived(ag_z(c, g))
        start(ag_xy(c, g))

    def users_of(g):
        return slice(g * U, (g + 1) * U)

    for g in range(GROUPS):
        for u in range(g * U // 128, (g + 1) * U // 128):
            picks = [chosen[u * 16 + k : u * 16 + k + 1] for k in range(CAP)]

            def block(b, carry, picks=picks, u=u):
                base = pl.multiple_of(b * 48, 48)
                at = (lax.broadcasted_iota(jnp.int32, (48, 128), 0) + base).astype(F32)
                hit = picks[0] == at
                for p in picks[1:]:
                    hit = hit | (p == at)
                s_sc[pl.ds(base, 48), u * 128 : (u + 1) * 128] = jnp.where(hit, 1.0, 0.0).astype(BF16)
                return carry

            lax.fori_loop(0, COLS // 48, block, 0)
        partial_inputs(0, g, s_sc[:, users_of(g)])
    for g in range(GROUPS):
        plane_sum(0, g)
    for g in range(GROUPS):
        pos_own[g] = ring_sum(0, g)
    for g in range(GROUPS):
        ring_gather(0, g)
    for g in range(GROUPS):
        arrived(ag_xy(0, g))
        l_sc[...] = dot(w_sc[...], hid[0, users_of(g)], 1, 1)

        def softmax(b, carry, g=g):
            base = pl.multiple_of(b * 16, 16)
            for h in range(U // 128):
                lanes = slice(h * 128, (h + 1) * 128)
                out_lanes = slice(g * U + h * 128, g * U + (h + 1) * 128)
                at = [pl.ds(pl.multiple_of(k * PAD + base, 16), 16) for k in range(LEVELS)]
                logits = [l_sc[a, lanes] + vbc[a, :] for a in at]
                largest = functools.reduce(jnp.maximum, logits)
                powers = [jnp.exp(v - largest) for v in logits]
                whole = functools.reduce(jnp.add, powers)
                rated = functools.reduce(jnp.add, [s_sc[a, out_lanes].astype(F32) for a in at])
                for a, v in zip(at, powers):
                    soft = (v / whole).astype(BF16)
                    r_sc[a, out_lanes] = (soft.astype(F32) * rated).astype(BF16)
            return carry

        lax.fori_loop(0, PAD // 16, softmax, 0)
        partial_inputs(1, g, r_sc[:, users_of(g)])

    ones = jnp.ones((8, USERS), BF16)
    vg_own = dot(ones, s_sc[...], 1, 1) - dot(ones, r_sc[...], 1, 1)
    vco[0] = vg_own
    vg_copy = pltpu.make_async_remote_copy(
        vco.at[0], vco.at[1], co_s.at[LEVELS], co_r.at[LEVELS], device_id=other, device_id_type=MESH
    )
    vg_copy.start()
    for k in range(LEVELS):
        acc_sc[k] = dot(s_sc[k * PAD : (k + 1) * PAD], hid[0], 1, 0)
    for u in range(4):
        at = pl.multiple_of(u * 128 + xy // 2 * 16, 16)
        block_rows = hid[0, pl.ds(at, 16), :].astype(F32)
        mine = lax.broadcasted_iota(jnp.int32, (16, F), 0) == lax.rem(xy, 2) * 8 + z
        ph_ref[u : u + 1] = jnp.sum(jnp.where(mine, block_rows, 0.0), axis=0, keepdims=True)

    for g in range(GROUPS):
        plane_sum(1, g)
    change = jnp.zeros((1, 128), F32)
    for g in range(GROUPS):
        value = ring_sum(1, g)
        change = change + jnp.sum(pos_own[g] - value, axis=0, keepdims=True)
    hz[z] = change
    h_z = z_copies(lambda t: hz.at[z], lambda d: hz.at[z], hz_s, hz_r)
    start(h_z)
    for g in range(GROUPS):
        ring_gather(1, g)
    arrived(h_z)
    hxy[xy] = hz[...]
    h_xy = xy_copies(lambda t: hxy.at[xy], lambda d: hxy.at[xy], hx_s, hx_r)
    start(h_xy)
    arrived(h_xy)
    total = hxy[0]
    for d in range(1, NXY):
        total = total + hxy[d]
    hco[0] = total
    hg_copy = pltpu.make_async_remote_copy(
        hco.at[0], hco.at[1], co_s.at[LEVELS + 1], co_r.at[LEVELS + 1], device_id=other, device_id_type=MESH
    )
    hg_copy.start()
    for g in range(GROUPS):
        arrived(ag_xy(1, g))

    wg_copies = []
    for k in range(LEVELS):
        grad = acc_sc[k] - dot(r_sc[k * PAD : (k + 1) * PAD], hid[1], 1, 0)
        own_sc[k] = grad.astype(BF16)
        copy = pltpu.make_async_remote_copy(
            own_sc.at[k], oth_sc.at[k], co_s.at[k], co_r.at[k], device_id=other, device_id_type=MESH
        )
        copy.start()
        wg_copies.append(copy)
    hg_copy.wait_recv()
    hg_ref[...] = hco[0] + hco[1]
    vg_copy.wait_recv()
    vg_ref[...] = vco[0] + vco[1]
    for k in range(LEVELS):
        wg_copies[k].wait_recv()
        wg_ref[k] = own_sc[k, 0:MOV].astype(F32) + oth_sc[k, 0:MOV].astype(F32)
    for c in range(2):
        for g in range(GROUPS):
            for copies in (rs_xy(c, g), rs_z(c, g), ag_z(c, g), ag_xy(c, g)):
                sent(copies)
    sent(h_z)
    sent(h_xy)
    for copy in (*wg_copies, hg_copy, vg_copy):
        copy.wait_send()


def on_device(movie_ids, ratings, valid, weights, vis_bias, hid_bias):
    dma = pltpu.SemaphoreType.DMA
    wg, vg, hg, ph = pl.pallas_call(
        kernel,
        out_shape=(
            jax.ShapeDtypeStruct((LEVELS, MOV, F), F32),
            jax.ShapeDtypeStruct((8, COLS), F32),
            jax.ShapeDtypeStruct((NZ, 1, 128), F32),
            jax.ShapeDtypeStruct((4, F), F32),
        ),
        in_specs=[pl.BlockSpec(memory_space=pltpu.VMEM)] * 6,
        out_specs=(pl.BlockSpec(memory_space=pltpu.VMEM),) * 4,
        scratch_shapes=[
            pltpu.VMEM((COLS, F), BF16),
            pltpu.VMEM((8, 256), F32),
            pltpu.VMEM((COLS, 128), F32),
            pltpu.VMEM((128, 128), F32),
            pltpu.VMEM((NZ, NXY, 1, 128), F32),
            pltpu.VMEM((NZ, NXY, 1, 128), F32),
            pltpu.VMEM((NXY, NZ, 1, 128), F32),
            pltpu.VMEM((COLS, USERS), BF16),
            pltpu.VMEM((COLS, USERS), BF16),
            pltpu.VMEM((COLS, U), F32),
            pltpu.VMEM((2, USERS, F), BF16),
            pltpu.VMEM((2, GROUPS, NXY, R, F), BF16),
            pltpu.VMEM((2, GROUPS, NZ, R, 128), BF16),
            pltpu.VMEM((2, GROUPS, NZ, R, 128), BF16),
            pltpu.VMEM((2, USERS, F), BF16),
            pltpu.VMEM((GROUPS, R, 128), F32),
            pltpu.VMEM((LEVELS, PAD, F), F32),
            pltpu.VMEM((LEVELS, PAD, F), BF16),
            pltpu.VMEM((LEVELS, PAD, F), BF16),
            pltpu.VMEM((NZ, 1, 128), F32),
            pltpu.VMEM((NXY, NZ, 1, 128), F32),
            pltpu.VMEM((2, NZ, 1, 128), F32),
            pltpu.VMEM((2, 8, COLS), F32),
            dma((NZ,)), dma((NZ,)), dma((NXY,)), dma((NXY,)),
            dma((4, GROUPS, NZ)), dma((4, GROUPS, NZ)), dma((4, GROUPS, NXY)), dma((4, GROUPS, NXY)),
            dma((NZ,)), dma((NZ,)), dma((NXY,)), dma((NXY,)),
            dma((LEVELS + 2,)), dma((LEVELS + 2,)),
        ],
        compiler_params=pltpu.CompilerParams(
            collective_id=0, has_side_effects=True, vmem_limit_bytes=50 << 20
        ),
    )(movie_ids, ratings, valid, weights, vis_bias, hid_bias.reshape(NZ, 1, 128))
    visible_grad = vg[0].reshape(LEVELS, PAD)[:, :MOV]
    return wg, visible_grad, hg.reshape(F), ph


def solution(mesh):
    split = Mesh(mesh.devices.reshape(NZ, 4, 4, mesh.shape["user"]), ALL)
    owner = ("z", "y", "x")
    in_specs = (P(ALL, None), P(ALL, None), P(ALL, None), P(None, owner, None), P(None, owner), P())
    out_specs = (P(None, owner, None), P(None, owner), P(), P(ALL, None))
    return jax.shard_map(on_device, mesh=split, in_specs=in_specs, out_specs=out_specs, check_vma=False)
```

```python
import functools

import jax
import jax.numpy as jnp
from jax import lax
from jax.experimental import pallas as pl
from jax.experimental.pallas import tpu as pltpu
from jax.sharding import Mesh
from jax.sharding import PartitionSpec as P

LEVELS = 5
MOV = 140
PAD = 144
COLS = LEVELS * PAD
F = 1024
NZ, NXY = 8, 16
CAP = 12
USERS = 512
GROUPS = 2
U = USERS // GROUPS
R = U // NXY
ALL = ("z", "y", "x", "core")
MESH = pl.DeviceIdType.MESH
F32, BF16 = jnp.float32, jnp.bfloat16


def dot(a, b, ca, cb):
    return lax.dot_general(a, b, (((ca,), (cb,)), ((), ())), preferred_element_type=F32)


def kernel(
    ids_hbm, rat_hbm, val_hbm, w_hbm, vb_hbm, hb_hbm,
    own_sc, oth_sc, vco, hco, ph_ref,
    ids_ref, rat_ref, val_ref, w_ref, vb_ref, hb_ref, in_sem,
    w_sc, vb_pad, vbc, t2d, t_send, d1, d2, s_sc, r_sc, l_sc,
    p_sc, r1, q_sc, r2, hid, pos_own, acc_sc, hz, hxy,
    dz_s, dz_r, dx_s, dx_r, cz_s, cz_r, cx_s, cx_r, hz_s, hz_r, hx_s, hx_r, co_s, co_r,
):
    z, y, x, core = [lax.axis_index(a) for a in ALL]
    xy = y * 4 + x
    other = (z, y, x, 1 - core)

    def xy_peer(d):
        return lax.rem(y + d // 4, 4), lax.rem(x + lax.rem(d, 4), 4)

    def z_peer(d):
        return lax.rem(z + d, NZ)

    def xy_copies(src, dst, send, recv):
        def copy(d):
            ty, tx = xy_peer(d)
            return pltpu.make_async_remote_copy(
                src(ty * 4 + tx), dst(d), send.at[d], recv.at[d],
                device_id=(z, ty, tx, core), device_id_type=MESH,
            )

        return NXY, copy

    def z_copies(src, dst, send, recv):
        def copy(d):
            tz = z_peer(d)
            return pltpu.make_async_remote_copy(
                src(tz), dst(d), send.at[d], recv.at[d],
                device_id=(tz, y, x, core), device_id_type=MESH,
            )

        return NZ, copy

    def each(copies, act):
        n, copy = copies

        def step(d, carry):
            act(copy(d))
            return carry

        lax.fori_loop(1, n, step, 0)

    started = []

    def start(copies):
        started.append(copies)
        each(copies, lambda c: c.start())

    def arrived(copies):
        each(copies, lambda c: c.wait_recv())

    def sent(copies):
        each(copies, lambda c: c.wait_send())

    inputs = [
        pltpu.make_async_copy(src, dst, in_sem.at[i])
        for i, (src, dst) in enumerate(
            (
                (ids_hbm, ids_ref), (rat_hbm, rat_ref), (val_hbm, val_ref),
                (w_hbm, w_ref), (vb_hbm, vb_ref), (hb_hbm, hb_ref),
            )
        )
    ]
    for copy in inputs:
        copy.start()

    barrier = pltpu.get_barrier_semaphore()

    def greet_xy(d, carry):
        ty, tx = xy_peer(d)
        pl.semaphore_signal(barrier, 1, device_id=(z, ty, tx, core), device_id_type=MESH)
        return carry

    def greet_z(d, carry):
        pl.semaphore_signal(barrier, 1, device_id=(z_peer(d), y, x, core), device_id_type=MESH)
        return carry

    lax.fori_loop(1, NZ, greet_z, 0)
    lax.fori_loop(1, NXY, greet_xy, 0)
    pl.semaphore_signal(barrier, 1, device_id=other, device_id_type=MESH)

    for copy in inputs[:3]:
        copy.wait()
    ids = ids_ref[...]
    owner = jnp.floor((ids.astype(F32) + 0.5) * (1.0 / MOV)).astype(jnp.int32)
    column = rat_ref[...] * PAD + (ids - owner * MOV) + 1
    high = lax.shift_right_logical(column, 5).astype(F32)
    low = (column & 31).astype(F32)
    owner = jnp.where(val_ref[...] == 1, owner, -1)
    row = lax.broadcasted_iota(jnp.int32, (128, 128), 0)
    lane = lax.broadcasted_iota(jnp.int32, (128, 128), 1)
    before = jnp.where(row < lane, 1.0, 0.0).astype(BF16)
    rank_row = (row & 15).astype(F32)
    user_row = lax.shift_right_logical(row, 4) & 3
    table = jnp.zeros((128, 128), F32)
    for u in range(4):
        hot = jnp.where(owner[u : u + 1] == row, 1.0, 0.0)
        hot_low = hot.astype(BF16)
        rank = jnp.sum(hot * dot(hot_low, before, 1, 0), axis=0, keepdims=True)
        part = jnp.where(row < 64, high[u : u + 1], low[u : u + 1])
        pick = jnp.where((user_row == u) & (rank_row == rank), part, 0.0)
        table = table + dot(hot_low, pick.astype(BF16), 1, 1)
    t2d[...] = table

    def spread(i, carry):
        t_send[i // NXY, lax.rem(i, NXY)] = t2d[pl.ds(i, 1), :]
        return carry

    lax.fori_loop(0, 128, spread, 0)

    for copy in inputs[3:]:
        copy.wait()
    for k in range(LEVELS):
        w_sc[k * PAD + 128 : (k + 1) * PAD] = jnp.zeros((PAD - 128, F), BF16)
        w_sc[k * PAD : k * PAD + MOV] = w_ref[k]
    vb_pad[...] = jnp.zeros((8, 256), F32)
    vb_pad[0:LEVELS, 0:MOV] = vb_ref[...]
    bias_columns = jnp.transpose(vb_pad[...])
    for k in range(LEVELS):
        vbc[k * PAD : (k + 1) * PAD] = jnp.broadcast_to(bias_columns[0:PAD, k : k + 1], (PAD, 128))

    pl.semaphore_wait(barrier, NZ - 1 + NXY - 1 + 1)

    to_z = z_copies(lambda t: t_send.at[t], lambda d: d1.at[z], dz_s, dz_r)
    start(to_z)
    d1[z] = t_send[z]
    arrived(to_z)
    to_xy = xy_copies(lambda t: d1.at[:, t], lambda d: d2.at[xy], dx_s, dx_r)
    start(to_xy)
    d2[xy] = d1[:, xy]
    arrived(to_xy)

    def collect(i, carry):
        t2d[pl.ds(i, 1), :] = d2[i // NZ, lax.rem(i, NZ)]
        return carry

    lax.fori_loop(0, 128, collect, 0)
    got = jnp.transpose(t2d[...])
    chosen = got[0:64] * 32.0 + got[64:128] - 1.0

    def group_rows(c, g, t):
        return hid.at[c, pl.ds(pl.multiple_of(g * U + t * R, R), R), :]

    @functools.cache
    def rs_xy(c, g):
        return xy_copies(
            lambda t: p_sc.at[c, pl.ds(pl.multiple_of(g * U + t * R, R), R), :],
            lambda d: r1.at[c, g, d], cx_s.at[2 * c, g], cx_r.at[2 * c, g],
        )

    @functools.cache
    def rs_z(c, g):
        return z_copies(
            lambda t: q_sc.at[c, g, t], lambda d: r2.at[c, g, d], cz_s.at[2 * c, g], cz_r.at[2 * c, g]
        )

    def own_piece(c, g):
        rows = pl.ds(pl.multiple_of(g * U + xy * R, R), R)
        return hid.at[c, rows, pl.ds(pl.multiple_of(z * 128, 128), 128)]

    @functools.cache
    def ag_z(c, g):
        return z_copies(
            lambda t: own_piece(c, g), lambda d: own_piece(c, g), cz_s.at[2 * c + 1, g], cz_r.at[2 * c + 1, g]
        )

    @functools.cache
    def ag_xy(c, g):
        return xy_copies(
            lambda t: group_rows(c, g, xy), lambda d: group_rows(c, g, xy),
            cx_s.at[2 * c + 1, g], cx_r.at[2 * c + 1, g],
        )

    def partial_inputs(c, g, visible):
        p_sc[c, g * U : (g + 1) * U] = dot(visible, w_sc[...], 0, 0).astype(BF16)
        start(rs_xy(c, g))

    def plane_sum(c, g):
        arrived(rs_xy(c, g))
        rows = pl.ds(pl.multiple_of(g * U + xy * R, R), R)
        for f in range(NZ):
            cut = slice(f * 128, (f + 1) * 128)
            total = p_sc[c, rows, cut].astype(F32)
            for d in range(1, NXY):
                total = total + r1[c, g, d, :, cut].astype(F32)
            q_sc[c, g, f] = total.astype(BF16)
        start(rs_z(c, g))

    def ring_sum(c, g):
        arrived(rs_z(c, g))
        total = q_sc[c, g, z].astype(F32)
        for d in range(1, NZ):
            total = total + r2[c, g, d].astype(F32)
        value = 1.0 / (1.0 + jnp.exp(-(total + hb_ref[z])))
        own_piece(c, g)[...] = value.astype(BF16)
        start(ag_z(c, g))
        return value

    def ring_gather(c, g):
        arrived(ag_z(c, g))
        start(ag_xy(c, g))

    def users_of(g):
        return slice(g * U, (g + 1) * U)

    for g in range(GROUPS):
        for u in range(g * U // 128, (g + 1) * U // 128):
            picks = [chosen[u * 16 + k : u * 16 + k + 1] for k in range(CAP)]

            def block(b, carry, picks=picks, u=u):
                base = pl.multiple_of(b * 48, 48)
                at = (lax.broadcasted_iota(jnp.int32, (48, 128), 0) + base).astype(F32)
                hit = picks[0] == at
                for p in picks[1:]:
                    hit = hit | (p == at)
                s_sc[pl.ds(base, 48), u * 128 : (u + 1) * 128] = jnp.where(hit, 1.0, 0.0).astype(BF16)
                return carry

            lax.fori_loop(0, COLS // 48, block, 0)
        partial_inputs(0, g, s_sc[:, users_of(g)])
    for g in range(GROUPS):
        plane_sum(0, g)
    for g in range(GROUPS):
        pos_own[g] = ring_sum(0, g)
    for g in range(GROUPS):
        ring_gather(0, g)
    for g in range(GROUPS):
        arrived(ag_xy(0, g))
        l_sc[...] = dot(w_sc[...], hid[0, users_of(g)], 1, 1)

        def softmax(b, carry, g=g):
            base = pl.multiple_of(b * 16, 16)
            for h in range(U // 128):
                lanes = slice(h * 128, (h + 1) * 128)
                out_lanes = slice(g * U + h * 128, g * U + (h + 1) * 128)
                at = [pl.ds(pl.multiple_of(k * PAD + base, 16), 16) for k in range(LEVELS)]
                logits = [l_sc[a, lanes] + vbc[a, :] for a in at]
                largest = functools.reduce(jnp.maximum, logits)
                powers = [jnp.exp(v - largest) for v in logits]
                whole = functools.reduce(jnp.add, powers)
                rated = functools.reduce(jnp.add, [s_sc[a, out_lanes].astype(F32) for a in at])
                for a, v in zip(at, powers):
                    soft = (v / whole).astype(BF16)
                    r_sc[a, out_lanes] = (soft.astype(F32) * rated).astype(BF16)
            return carry

        lax.fori_loop(0, PAD // 16, softmax, 0)
        partial_inputs(1, g, r_sc[:, users_of(g)])

    ones = jnp.ones((8, USERS), BF16)
    for k in range(LEVELS):
        level = slice(k * PAD, (k + 1) * PAD)
        moved = dot(ones, s_sc[level], 1, 1) - dot(ones, r_sc[level], 1, 1)
        vco[0, k : k + 1] = moved[0:1]
    vg_copy = pltpu.make_async_remote_copy(
        vco.at[0], vco.at[1], co_s.at[LEVELS], co_r.at[LEVELS], device_id=other, device_id_type=MESH
    )
    vg_copy.start()
    for k in range(LEVELS):
        acc_sc[k] = dot(s_sc[k * PAD : (k + 1) * PAD], hid[0], 1, 0)
    for u in range(4):
        at = pl.multiple_of(u * 128 + xy // 2 * 16, 16)
        block_rows = hid[0, pl.ds(at, 16), :].astype(F32)
        mine = lax.broadcasted_iota(jnp.int32, (16, F), 0) == lax.rem(xy, 2) * 8 + z
        ph_ref[u : u + 1] = jnp.sum(jnp.where(mine, block_rows, 0.0), axis=0, keepdims=True)

    for g in range(GROUPS):
        plane_sum(1, g)
    change = jnp.zeros((1, 128), F32)
    for g in range(GROUPS):
        value = ring_sum(1, g)
        change = change + jnp.sum(pos_own[g] - value, axis=0, keepdims=True)
    hz[z] = change
    h_z = z_copies(lambda t: hz.at[z], lambda d: hz.at[z], hz_s, hz_r)
    start(h_z)
    for g in range(GROUPS):
        ring_gather(1, g)
    arrived(h_z)
    hxy[xy] = hz[...]
    h_xy = xy_copies(lambda t: hxy.at[xy], lambda d: hxy.at[xy], hx_s, hx_r)
    start(h_xy)
    arrived(h_xy)
    total = hxy[0]
    for d in range(1, NXY):
        total = total + hxy[d]
    hco[0] = total
    hg_copy = pltpu.make_async_remote_copy(
        hco.at[0], hco.at[1], co_s.at[LEVELS + 1], co_r.at[LEVELS + 1], device_id=other, device_id_type=MESH
    )
    hg_copy.start()
    for g in range(GROUPS):
        arrived(ag_xy(1, g))

    wg_copies = []
    for k in range(LEVELS):
        grad = acc_sc[k] - dot(r_sc[k * PAD : (k + 1) * PAD], hid[1], 1, 0)
        own_sc[k] = grad.astype(BF16)
        copy = pltpu.make_async_remote_copy(
            own_sc.at[k], oth_sc.at[k], co_s.at[k], co_r.at[k], device_id=other, device_id_type=MESH
        )
        copy.start()
        wg_copies.append(copy)
    for copy in (hg_copy, vg_copy, *wg_copies):
        copy.wait_recv()
    for copies in started:
        sent(copies)
    for copy in (*wg_copies, hg_copy, vg_copy):
        copy.wait_send()


def finish(own_ref, oth_ref, vco_ref, hco_ref, ph_ref, wg_out, vg_out, hg_out, ph_out, wg, vg, hg, sem):
    copies = []
    for i, (src, dst) in enumerate(((ph_ref, ph_out), (vg, vg_out), (hg, hg_out))):
        copies.append(pltpu.make_async_copy(src, dst, sem.at[i]))
    copies[0].start()
    vg[...] = (vco_ref[0] + vco_ref[1])[0:LEVELS, 0:MOV]
    copies[1].start()
    hg[...] = hco_ref[0] + hco_ref[1]
    copies[2].start()
    for k in range(LEVELS):
        wg[k] = own_ref[k, 0:MOV].astype(F32) + oth_ref[k, 0:MOV].astype(F32)
        copies.append(pltpu.make_async_copy(wg.at[k], wg_out.at[k], sem.at[3 + k]))
        copies[-1].start()
    for copy in copies:
        copy.wait()


def on_device(movie_ids, ratings, valid, weights, vis_bias, hid_bias):
    dma = pltpu.SemaphoreType.DMA
    vmem = pl.BlockSpec(memory_space=pltpu.VMEM)
    hbm = pl.BlockSpec(memory_space=pltpu.HBM)
    shape = jax.ShapeDtypeStruct
    parts = pl.pallas_call(
        kernel,
        out_shape=(
            shape((LEVELS, PAD, F), BF16),
            shape((LEVELS, PAD, F), BF16),
            shape((2, 8, PAD), F32),
            shape((2, NZ, 1, 128), F32),
            shape((4, F), F32),
        ),
        in_specs=[hbm] * 6,
        out_specs=(vmem,) * 5,
        scratch_shapes=[
            pltpu.VMEM((4, 128), jnp.int32), pltpu.VMEM((4, 128), jnp.int32), pltpu.VMEM((4, 128), jnp.int32),
            pltpu.VMEM((LEVELS, MOV, F), BF16), pltpu.VMEM((LEVELS, MOV), F32), pltpu.VMEM((NZ, 1, 128), F32),
            dma((6,)),
            pltpu.VMEM((COLS, F), BF16),
            pltpu.VMEM((8, 256), F32),
            pltpu.VMEM((COLS, 128), F32),
            pltpu.VMEM((128, 128), F32),
            pltpu.VMEM((NZ, NXY, 1, 128), F32),
            pltpu.VMEM((NZ, NXY, 1, 128), F32),
            pltpu.VMEM((NXY, NZ, 1, 128), F32),
            pltpu.VMEM((COLS, USERS), BF16),
            pltpu.VMEM((COLS, USERS), BF16),
            pltpu.VMEM((COLS, U), F32),
            pltpu.VMEM((2, USERS, F), BF16),
            pltpu.VMEM((2, GROUPS, NXY, R, F), BF16),
            pltpu.VMEM((2, GROUPS, NZ, R, 128), BF16),
            pltpu.VMEM((2, GROUPS, NZ, R, 128), BF16),
            pltpu.VMEM((2, USERS, F), BF16),
            pltpu.VMEM((GROUPS, R, 128), F32),
            pltpu.VMEM((LEVELS, PAD, F), F32),
            pltpu.VMEM((NZ, 1, 128), F32),
            pltpu.VMEM((NXY, NZ, 1, 128), F32),
            dma((NZ,)), dma((NZ,)), dma((NXY,)), dma((NXY,)),
            dma((4, GROUPS, NZ)), dma((4, GROUPS, NZ)), dma((4, GROUPS, NXY)), dma((4, GROUPS, NXY)),
            dma((NZ,)), dma((NZ,)), dma((NXY,)), dma((NXY,)),
            dma((LEVELS + 2,)), dma((LEVELS + 2,)),
        ],
        compiler_params=pltpu.CompilerParams(
            collective_id=0, has_side_effects=True, vmem_limit_bytes=36 << 20
        ),
    )(*[
        pltpu.with_memory_space_constraint(a, pltpu.HBM)
        for a in (movie_ids, ratings, valid, weights, vis_bias, hid_bias.reshape(NZ, 1, 128))
    ])
    wg, vg, hg, ph = pl.pallas_call(
        finish,
        out_shape=(shape((LEVELS, MOV, F), F32), shape((LEVELS, MOV), F32), shape((NZ, 1, 128), F32), shape((4, F), F32)),
        in_specs=[vmem] * 5,
        out_specs=(hbm,) * 4,
        scratch_shapes=[
            pltpu.VMEM((LEVELS, MOV, F), F32), pltpu.VMEM((LEVELS, MOV), F32), pltpu.VMEM((NZ, 1, 128), F32), dma((8,)),
        ],
        compiler_params=pltpu.CompilerParams(vmem_limit_bytes=8 << 20),
    )(*parts)
    return wg, vg, hg.reshape(F), ph


def solution(mesh):
    split = Mesh(mesh.devices.reshape(NZ, 4, 4, mesh.shape["user"]), ALL)
    owner = ("z", "y", "x")
    in_specs = (P(ALL, None), P(ALL, None), P(ALL, None), P(None, owner, None), P(None, owner), P())
    out_specs = (P(None, owner, None), P(None, owner), P(), P(ALL, None))
    return jax.shard_map(on_device, mesh=split, in_specs=in_specs, out_specs=out_specs, check_vma=False)
```

```python
import functools

import jax
import jax.numpy as jnp
from jax import lax
from jax.experimental import pallas as pl
from jax.experimental.pallas import tpu as pltpu
from jax.sharding import Mesh
from jax.sharding import PartitionSpec as P

LEVELS = 5
MOV = 140
PAD = 144
COLS = LEVELS * PAD
F = 1024
NZ, NXY = 8, 16
CAP = 12
USERS = 512
BLOCKS = USERS // 8
GROUPS = ((0, 128, True), (128, 128, False), (256, 128, False), (384, 128, False))
SUM_ORDER = (0, 1, 2, 3)
BATCHES = ((0, 1), (2, 3))
MOST = max(n for _, n, _ in GROUPS)
WIDEST = 256
ALL = ("z", "y", "x", "core")
MESH = pl.DeviceIdType.MESH
F32, BF16 = jnp.float32, jnp.bfloat16


def dot(a, b, ca, cb):
    return lax.dot_general(a, b, (((ca,), (cb,)), ((), ())), preferred_element_type=F32)


def kernel(
    ids_hbm, rat_hbm, val_hbm, w_hbm, vb_hbm, hb_hbm,
    own_sc, oth_sc, vco, hco, ph_ref,
    ids_ref, rat_ref, val_ref, w_ref, vb_ref, hb_ref, in_sem,
    w_sc, vb_pad, vbc, t2d, t_send, d1, d2, s_sc, r_sc, l_sc,
    p_sc, r1, q_sc, r2, hid, flat, pos_own, acc_sc, hz, hxy,
    dz_s, dz_r, dx_s, dx_r, cz_s, cz_r, cx_s, cx_r, hz_s, hz_r, hx_s, hx_r, co_s, co_r,
):
    z, y, x, core = [lax.axis_index(a) for a in ALL]
    xy = y * 4 + x
    other = (z, y, x, 1 - core)

    def xy_peer(d):
        return lax.rem(y + d // 4, 4), lax.rem(x + lax.rem(d, 4), 4)

    def z_peer(d):
        return lax.rem(z + d, NZ)

    def xy_copies(src, dst, send, recv, whole):
        def copy(d):
            ty, tx = xy_peer(d)
            return pltpu.make_async_remote_copy(
                src(ty * 4 + tx), dst(d), send, recv, device_id=(z, ty, tx, core), device_id_type=MESH
            )

        return NXY, copy, send, recv, whole

    def z_copies(src, dst, send, recv, whole):
        def copy(d):
            tz = z_peer(d)
            return pltpu.make_async_remote_copy(
                src(tz), dst(d), send, recv, device_id=(tz, y, x, core), device_id_type=MESH
            )

        return NZ, copy, send, recv, whole

    started = []

    def start(copies):
        started.append(copies)
        n, copy = copies[:2]

        def step(d, carry):
            copy(d).start()
            return carry

        lax.fori_loop(1, n, step, 0)

    def all_of(copies):
        send, recv, whole = copies[2:]
        return pltpu.make_async_remote_copy(whole, whole, send, recv, device_id=other, device_id_type=MESH)

    def arrived(copies):
        all_of(copies).wait_recv()

    def sent(copies):
        all_of(copies).wait_send()

    inputs = [
        pltpu.make_async_copy(src, dst, in_sem.at[i])
        for i, (src, dst) in enumerate(
            (
                (ids_hbm, ids_ref), (rat_hbm, rat_ref), (val_hbm, val_ref),
                (w_hbm, w_ref), (vb_hbm, vb_ref), (hb_hbm, hb_ref),
            )
        )
    ]
    for copy in inputs:
        copy.start()

    barrier = pltpu.get_barrier_semaphore()

    def greet_xy(d, carry):
        ty, tx = xy_peer(d)
        pl.semaphore_signal(barrier, 1, device_id=(z, ty, tx, core), device_id_type=MESH)
        return carry

    def greet_z(d, carry):
        pl.semaphore_signal(barrier, 1, device_id=(z_peer(d), y, x, core), device_id_type=MESH)
        return carry

    lax.fori_loop(1, NZ, greet_z, 0)
    lax.fori_loop(1, NXY, greet_xy, 0)
    pl.semaphore_signal(barrier, 1, device_id=other, device_id_type=MESH)

    for copy in inputs[:3]:
        copy.wait()
    ids = ids_ref[...]
    owner = jnp.floor((ids.astype(F32) + 0.5) * (1.0 / MOV)).astype(jnp.int32)
    column = rat_ref[...] * PAD + (ids - owner * MOV) + 1
    high = lax.shift_right_logical(column, 5).astype(F32)
    low = (column & 31).astype(F32)
    owner = jnp.where(val_ref[...] == 1, owner, -1)
    row = lax.broadcasted_iota(jnp.int32, (128, 128), 0)
    lane = lax.broadcasted_iota(jnp.int32, (128, 128), 1)
    before = jnp.where(row < lane, 1.0, 0.0).astype(BF16)
    rank_row = (row & 15).astype(F32)
    user_row = lax.shift_right_logical(row, 4) & 3
    hot = [jnp.where(owner[u : u + 1] == row, 1.0, 0.0) for u in range(4)]
    counts = dot(jnp.concatenate(hot, axis=0).astype(BF16), before, 1, 0)
    picks = []
    for u in range(4):
        rank = jnp.sum(hot[u] * counts[u * 128 : (u + 1) * 128], axis=0, keepdims=True)
        part = jnp.where(row < 64, high[u : u + 1], low[u : u + 1])
        picks.append(jnp.where((user_row == u) & (rank_row == rank), part, 0.0))
    table = dot(
        jnp.concatenate(hot, axis=1).astype(BF16), jnp.concatenate(picks, axis=1).astype(BF16), 1, 1
    )
    for i in range(NZ):
        for k in range(NXY):
            t_send[i, k] = table[i * NXY + k : i * NXY + k + 1]

    pl.semaphore_wait(barrier, NZ - 1 + NXY - 1 + 1)

    to_z = z_copies(
        lambda t: t_send.at[t], lambda d: d1.at[z], dz_s.at[0], dz_r.at[0], t_send.at[0 : NZ - 1]
    )
    start(to_z)
    d1[z] = t_send[z]
    for copy in inputs[3:]:
        copy.wait()
    for k in range(LEVELS):
        w_sc[k * PAD + 128 : (k + 1) * PAD] = jnp.zeros((PAD - 128, F), BF16)
        w_sc[k * PAD : k * PAD + MOV] = w_ref[k]
    vb_pad[...] = jnp.zeros((8, 256), F32)
    vb_pad[0:LEVELS, 0:MOV] = vb_ref[...]
    bias_columns = jnp.transpose(vb_pad[...])
    for k in range(LEVELS):
        vbc[k * PAD : (k + 1) * PAD] = jnp.broadcast_to(bias_columns[0:PAD, k : k + 1], (PAD, 128))

    arrived(to_z)
    to_xy = xy_copies(
        lambda t: d1.at[:, t], lambda d: d2.at[xy], dx_s.at[0], dx_r.at[0], d2.at[0 : NXY - 1]
    )
    start(to_xy)
    d2[xy] = d1[:, xy]
    arrived(to_xy)

    for i in range(NXY):
        for k in range(NZ):
            t2d[i * NZ + k : i * NZ + k + 1] = d2[i, k]
    got = jnp.transpose(t2d[...])
    chosen = got[0:64] * 32.0 + got[64:128] - 1.0

    def layout(g):
        first, users, ring_first = GROUPS[g]
        return first // 8, users // 128, ring_first

    def piece(t, g, first_stage):
        base, n, ring_first = layout(g)
        return pl.ds(base + t * n * (2 if ring_first and first_stage else 1), n * (2 if ring_first and first_stage else 1))

    def own_blocks(g):
        return piece(z if layout(g)[2] else xy, g, True)

    def own_chunk(g):
        return lax.rem(xy, NZ) if layout(g)[2] else z

    def own_piece(c, g):
        base, n, ring_first = layout(g)
        blocks = pl.ds(base + (z * 2 + xy // NZ) * n, n) if ring_first else own_blocks(g)
        return hid.at[c, blocks, :, pl.ds(pl.multiple_of(own_chunk(g) * 128, 128), 128)]

    def stage(c, half, g, is_wide, src, dst):
        k, ring = 2 * c + half, layout(g)[2] == is_wide
        base, n, _ = layout(g)
        count = (NZ if ring else NXY) - 1
        rows = n * (2 if layout(g)[2] else 1)
        whole = p_sc.at[c, pl.ds(base, count * rows)] if is_wide else q_sc.at[c, g, 0:count, 0:n]
        if ring:
            return z_copies(src, dst, cz_s.at[k, g], cz_r.at[k, g], whole)
        return xy_copies(src, dst, cx_s.at[k, g], cx_r.at[k, g], whole)

    @functools.cache
    def rs_wide(c, g):
        return stage(c, 0, g, True, lambda t: p_sc.at[c, piece(t, g, True)], lambda d: r1.at[c, piece(d, g, True)])

    @functools.cache
    def rs_narrow(c, g):
        n = layout(g)[1]
        return stage(c, 0, g, False, lambda t: q_sc.at[c, g, t, 0:n], lambda d: r2.at[c, g, d, 0:n])

    @functools.cache
    def ag_narrow(c, g):
        return stage(c, 1, g, False, lambda t: own_piece(c, g), lambda d: own_piece(c, g))

    @functools.cache
    def ag_wide(c, g):
        return stage(c, 1, g, True, lambda t: hid.at[c, own_blocks(g)], lambda d: hid.at[c, own_blocks(g)])

    def users_of(g):
        first, users, _ = GROUPS[g]
        return slice(first, first + users)

    def blocks_of(g):
        first, users, _ = GROUPS[g]
        return slice(first // 8, (first + users) // 8)

    def batch_users(b):
        return slice(users_of(b[0]).start, users_of(b[-1]).stop)

    def partial_inputs(c, b, visible):
        sums = dot(visible, w_sc[...], 0, 0)
        first = batch_users(b).start // 8
        p_sc[c, first : first + sums.shape[0] // 8] = sums.reshape(sums.shape[0] // 8, 8, F).astype(BF16)
        for g in b:
            start(rs_wide(c, g))

    def first_sum(c, g):
        arrived(rs_wide(c, g))
        n, ring_first = layout(g)[1:]
        for h in range(2 if ring_first else 1):
            for f in range(NZ):
                cut = slice(f * 128, (f + 1) * 128)
                base = layout(g)[0]
                mine = base + (z * 2 * n if ring_first else xy * n) + h * n
                total = p_sc[c, pl.ds(mine, n), :, cut].astype(F32)
                for d in range(1, NZ if ring_first else NXY):
                    slot = base + d * n * (2 if ring_first else 1) + h * n
                    total = total + r1[c, slot : slot + n, :, cut].astype(F32)
                q_sc[c, g, h * NZ + f, 0:n] = total.astype(BF16)
        start(rs_narrow(c, g))

    def second_sum(c, g):
        arrived(rs_narrow(c, g))
        n, ring_first = layout(g)[1:]
        total = q_sc[c, g, xy if ring_first else z, 0:n].astype(F32)
        for d in range(1, NXY if ring_first else NZ):
            total = total + r2[c, g, d, 0:n].astype(F32)
        value = 1.0 / (1.0 + jnp.exp(-(total + hb_ref[own_chunk(g)])))
        own_piece(c, g)[...] = value.astype(BF16)
        start(ag_narrow(c, g))
        return value

    def gather(c, g):
        arrived(ag_narrow(c, g))
        start(ag_wide(c, g))

    def gathered(c, g):
        arrived(ag_wide(c, g))
        rows = hid[c, blocks_of(g)].astype(F32)
        flat[c, users_of(g)] = rows.reshape(rows.shape[0] * 8, F).astype(BF16)

    for b in BATCHES:
        for u in range(batch_users(b).start // 128, batch_users(b).stop // 128):
            picks = [chosen[u * 16 + k : u * 16 + k + 1] for k in range(CAP)]

            def block(b, carry, picks=picks, u=u):
                base = pl.multiple_of(b * 48, 48)
                at = (lax.broadcasted_iota(jnp.int32, (48, 128), 0) + base).astype(F32)
                hit = picks[0] == at
                for p in picks[1:]:
                    hit = hit | (p == at)
                s_sc[pl.ds(base, 48), u * 128 : (u + 1) * 128] = jnp.where(hit, 1.0, 0.0).astype(BF16)
                return carry

            lax.fori_loop(0, COLS // 48, block, 0)
        partial_inputs(0, b, s_sc[:, batch_users(b)])
    for g in SUM_ORDER:
        first_sum(0, g)
    for g in SUM_ORDER:
        pos_own[g, 0 : layout(g)[1]] = second_sum(0, g)
    for g in SUM_ORDER:
        gather(0, g)
    for b in BATCHES:
        for g in b:
            gathered(0, g)
        first = batch_users(b).start
        users = batch_users(b).stop - first
        l_sc[:, 0:users] = dot(w_sc[...], flat[0, batch_users(b)], 1, 1)

        def softmax(i, carry, first=first, users=users):
            base = pl.multiple_of(i * 16, 16)
            for h in range(users // 128):
                lanes = slice(h * 128, (h + 1) * 128)
                out_lanes = slice(first + h * 128, first + (h + 1) * 128)
                at = [pl.ds(pl.multiple_of(k * PAD + base, 16), 16) for k in range(LEVELS)]
                logits = [l_sc[a, lanes] + vbc[a, :] for a in at]
                largest = functools.reduce(jnp.maximum, logits)
                powers = [jnp.exp(v - largest) for v in logits]
                whole = functools.reduce(jnp.add, powers)
                rated = functools.reduce(jnp.add, [s_sc[a, out_lanes].astype(F32) for a in at])
                scale = rated / whole
                for a, v in zip(at, powers):
                    r_sc[a, out_lanes] = (v * scale).astype(BF16)
            return carry

        lax.fori_loop(0, PAD // 16, softmax, 0)
        partial_inputs(1, b, r_sc[:, batch_users(b)])

    ones = jnp.ones((8, USERS), BF16)
    for k in range(LEVELS):
        level = slice(k * PAD, (k + 1) * PAD)
        moved = dot(ones, s_sc[level], 1, 1) - dot(ones, r_sc[level], 1, 1)
        vco[0, k : k + 1] = moved[0:1]
    vg_copy = pltpu.make_async_remote_copy(
        vco.at[0], vco.at[1], co_s.at[LEVELS], co_r.at[LEVELS], device_id=other, device_id_type=MESH
    )
    vg_copy.start()
    for k in range(LEVELS):
        acc_sc[k] = dot(s_sc[k * PAD : (k + 1) * PAD], flat[0], 1, 0)
    for u in range(4):
        block_rows = hid[0, u * 16 + xy].astype(F32)
        mine = lax.broadcasted_iota(jnp.int32, (8, F), 0) == z
        ph_ref[u : u + 1] = jnp.sum(jnp.where(mine, block_rows, 0.0), axis=0, keepdims=True)

    for g in SUM_ORDER:
        first_sum(1, g)
    change = [jnp.zeros((1, 128), F32), jnp.zeros((1, 128), F32)]
    for g in SUM_ORDER:
        value = second_sum(1, g)
        kind = 1 if layout(g)[2] else 0
        moved = jnp.sum(pos_own[g, 0 : layout(g)[1]] - value, axis=0)
        change[kind] = change[kind] + jnp.sum(moved, axis=0, keepdims=True)
    hz[z] = jnp.concatenate(change, axis=0)
    h_z = z_copies(lambda t: hz.at[z], lambda d: hz.at[z], hz_s.at[0], hz_r.at[0], hz.at[0 : NZ - 1])
    start(h_z)
    for g in SUM_ORDER:
        gather(1, g)
    arrived(h_z)
    rest = functools.reduce(jnp.add, [hz[k, 1:2] for k in range(NZ)])
    for k in range(NZ):
        hxy[xy, k] = hz[k, 0:1] + jnp.where(lax.rem(xy, NZ) == k, rest, 0.0)
    h_xy = xy_copies(
        lambda t: hxy.at[xy], lambda d: hxy.at[xy], hx_s.at[0], hx_r.at[0], hxy.at[0 : NXY - 1]
    )
    start(h_xy)
    arrived(h_xy)
    total = hxy[0]
    for d in range(1, NXY):
        total = total + hxy[d]
    hco[0] = total
    hg_copy = pltpu.make_async_remote_copy(
        hco.at[0], hco.at[1], co_s.at[LEVELS + 1], co_r.at[LEVELS + 1], device_id=other, device_id_type=MESH
    )
    hg_copy.start()
    for g in SUM_ORDER:
        gathered(1, g)

    wg_copies = []
    for k in range(LEVELS):
        grad = acc_sc[k] - dot(r_sc[k * PAD : (k + 1) * PAD], flat[1], 1, 0)
        own_sc[k] = grad.astype(BF16)
        copy = pltpu.make_async_remote_copy(
            own_sc.at[k], oth_sc.at[k], co_s.at[k], co_r.at[k], device_id=other, device_id_type=MESH
        )
        copy.start()
        wg_copies.append(copy)
    for copy in (hg_copy, vg_copy, *wg_copies):
        copy.wait_recv()
    for copies in started:
        sent(copies)
    for copy in (*wg_copies, hg_copy, vg_copy):
        copy.wait_send()


def finish(own_ref, oth_ref, vco_ref, hco_ref, ph_ref, wg_out, vg_out, hg_out, ph_out, wg, vg, hg, sem):
    copies = []
    for i, (src, dst) in enumerate(((ph_ref, ph_out), (vg, vg_out), (hg, hg_out))):
        copies.append(pltpu.make_async_copy(src, dst, sem.at[i]))
    copies[0].start()
    vg[...] = (vco_ref[0] + vco_ref[1])[0:LEVELS, 0:MOV]
    copies[1].start()
    hg[...] = hco_ref[0] + hco_ref[1]
    copies[2].start()
    for k in range(LEVELS):
        wg[k] = own_ref[k, 0:MOV].astype(F32) + oth_ref[k, 0:MOV].astype(F32)
        copies.append(pltpu.make_async_copy(wg.at[k], wg_out.at[k], sem.at[3 + k]))
        copies[-1].start()
    for copy in copies:
        copy.wait()


def on_device(movie_ids, ratings, valid, weights, vis_bias, hid_bias):
    dma = pltpu.SemaphoreType.DMA
    vmem = pl.BlockSpec(memory_space=pltpu.VMEM)
    hbm = pl.BlockSpec(memory_space=pltpu.HBM)
    shape = jax.ShapeDtypeStruct
    parts = pl.pallas_call(
        kernel,
        out_shape=(
            shape((LEVELS, PAD, F), BF16),
            shape((LEVELS, PAD, F), BF16),
            shape((2, 8, PAD), F32),
            shape((2, NZ, 1, 128), F32),
            shape((4, F), F32),
        ),
        in_specs=[hbm] * 6,
        out_specs=(vmem,) * 5,
        scratch_shapes=[
            pltpu.VMEM((4, 128), jnp.int32), pltpu.VMEM((4, 128), jnp.int32), pltpu.VMEM((4, 128), jnp.int32),
            pltpu.VMEM((LEVELS, MOV, F), BF16), pltpu.VMEM((LEVELS, MOV), F32), pltpu.VMEM((NZ, 1, 128), F32),
            dma((6,)),
            pltpu.VMEM((COLS, F), BF16),
            pltpu.VMEM((8, 256), F32),
            pltpu.VMEM((COLS, 128), F32),
            pltpu.VMEM((128, 128), F32),
            pltpu.VMEM((NZ, NXY, 1, 128), F32),
            pltpu.VMEM((NZ, NXY, 1, 128), F32),
            pltpu.VMEM((NXY, NZ, 1, 128), F32),
            pltpu.VMEM((COLS, USERS), BF16),
            pltpu.VMEM((COLS, USERS), BF16),
            pltpu.VMEM((COLS, WIDEST), F32),
            pltpu.VMEM((2, BLOCKS, 8, F), BF16),
            pltpu.VMEM((2, BLOCKS, 8, F), BF16),
            pltpu.VMEM((2, len(GROUPS), NXY, MOST // 128, 8, 128), BF16),
            pltpu.VMEM((2, len(GROUPS), NXY, MOST // 128, 8, 128), BF16),
            pltpu.VMEM((2, BLOCKS, 8, F), BF16),
            pltpu.VMEM((2, USERS, F), BF16),
            pltpu.VMEM((len(GROUPS), MOST // 128, 8, 128), F32),
            pltpu.VMEM((LEVELS, PAD, F), F32),
            pltpu.VMEM((NZ, 2, 128), F32),
            pltpu.VMEM((NXY, NZ, 1, 128), F32),
            *[dma((1,))] * 4, *[dma((4, len(GROUPS)))] * 4, *[dma((1,))] * 4,
            dma((LEVELS + 2,)), dma((LEVELS + 2,)),
        ],
        compiler_params=pltpu.CompilerParams(
            collective_id=0, has_side_effects=True, vmem_limit_bytes=36 << 20
        ),
    )(*[
        pltpu.with_memory_space_constraint(a, pltpu.HBM)
        for a in (movie_ids, ratings, valid, weights, vis_bias, hid_bias.reshape(NZ, 1, 128))
    ])
    wg, vg, hg, ph = pl.pallas_call(
        finish,
        out_shape=(shape((LEVELS, MOV, F), F32), shape((LEVELS, MOV), F32), shape((NZ, 1, 128), F32), shape((4, F), F32)),
        in_specs=[vmem] * 5,
        out_specs=(hbm,) * 4,
        scratch_shapes=[
            pltpu.VMEM((LEVELS, MOV, F), F32), pltpu.VMEM((LEVELS, MOV), F32), pltpu.VMEM((NZ, 1, 128), F32), dma((8,)),
        ],
        compiler_params=pltpu.CompilerParams(vmem_limit_bytes=8 << 20),
    )(*parts)
    return wg, vg, hg.reshape(F), ph


def solution(mesh):
    split = Mesh(mesh.devices.reshape(NZ, 4, 4, mesh.shape["user"]), ALL)
    owner = ("z", "y", "x")
    in_specs = (P(ALL, None), P(ALL, None), P(ALL, None), P(None, owner, None), P(None, owner), P())
    out_specs = (P(None, owner, None), P(None, owner), P(), P(ALL, None))
    return jax.shard_map(on_device, mesh=split, in_specs=in_specs, out_specs=out_specs, check_vma=False)
```

```python
import functools

import jax
import jax.numpy as jnp
from jax import lax
from jax.experimental import pallas as pl
from jax.experimental.pallas import tpu as pltpu
from jax.sharding import Mesh
from jax.sharding import PartitionSpec as P

LEVELS = 5
MOV = 140
PAD = 144
COLS = LEVELS * PAD
F = 1024
NZ, NXY = 8, 16
CAP = 12
USERS = 512
BLOCKS = USERS // 8
GROUPS = ((0, 128, True), (128, 128, False), (256, 128, False), (384, 128, False))
SUM_ORDER = (0, 1, 2, 3)
PIPE = ((0, 1), (0, 0), (0, 2), (1, 1), (0, 3), (1, 0), (1, 2), (2, 1), (1, 3), (2, 0), (2, 2), (2, 3))
BATCHES = ((0, 1), (2, 3))
MOST = max(n for _, n, _ in GROUPS)
WIDEST = 256
ALL = ("z", "y", "x", "core")
MESH = pl.DeviceIdType.MESH
F32, BF16 = jnp.float32, jnp.bfloat16


def dot(a, b, ca, cb):
    return lax.dot_general(a, b, (((ca,), (cb,)), ((), ())), preferred_element_type=F32)


def kernel(
    ids_hbm, rat_hbm, val_hbm, w_hbm, vb_hbm, hb_hbm,
    wg_ref, vg_ref, hco, ph_ref,
    ids_ref, rat_ref, val_ref, w_ref, vb_ref, hb_ref, in_sem,
    w_sc, vb_pad, vbc, t2d, t_send, d1, d2, s_sc, r_sc, l_sc,
    p_sc, r1, q_sc, r2, hid, flat, pos_own, acc_sc, hz, hxy,
    dz_s, dz_r, dx_s, dx_r, cz_s, cz_r, cx_s, cx_r, hz_s, hz_r, hx_s, hx_r, hc_s, hc_r, co_s, co_r,
):
    z, y, x, core = [lax.axis_index(a) for a in ALL]
    xy = y * 4 + x
    other = (z, y, x, 1 - core)

    def xy_peer(d):
        return lax.rem(y + d // 4, 4), lax.rem(x + lax.rem(d, 4), 4)

    def z_peer(d):
        return lax.rem(z + d, NZ)

    def xy_copies(src, dst, send, recv, whole):
        def copy(d):
            ty, tx = xy_peer(d)
            return pltpu.make_async_remote_copy(
                src(ty * 4 + tx), dst(d), send, recv, device_id=(z, ty, tx, core), device_id_type=MESH
            )

        return NXY, copy, send, recv, whole

    def z_copies(src, dst, send, recv, whole):
        def copy(d):
            tz = z_peer(d)
            return pltpu.make_async_remote_copy(
                src(tz), dst(d), send, recv, device_id=(tz, y, x, core), device_id_type=MESH
            )

        return NZ, copy, send, recv, whole

    started = []

    def start(copies):
        started.append(copies)
        n, copy = copies[:2]

        def step(d, carry):
            copy(d).start()
            return carry

        lax.fori_loop(1, n, step, 0)

    def all_of(copies):
        send, recv, whole = copies[2:]
        return pltpu.make_async_remote_copy(whole, whole, send, recv, device_id=other, device_id_type=MESH)

    def arrived(copies):
        all_of(copies).wait_recv()

    def sent(copies):
        all_of(copies).wait_send()

    inputs = [
        pltpu.make_async_copy(src, dst, in_sem.at[i])
        for i, (src, dst) in enumerate(
            (
                (ids_hbm, ids_ref), (rat_hbm, rat_ref), (val_hbm, val_ref),
                (w_hbm, w_ref), (vb_hbm, vb_ref), (hb_hbm, hb_ref),
            )
        )
    ]
    for copy in inputs:
        copy.start()

    barrier = pltpu.get_barrier_semaphore()

    def greet_xy(d, carry):
        ty, tx = xy_peer(d)
        pl.semaphore_signal(barrier, 1, device_id=(z, ty, tx, core), device_id_type=MESH)
        return carry

    def greet_z(d, carry):
        pl.semaphore_signal(barrier, 1, device_id=(z_peer(d), y, x, core), device_id_type=MESH)
        return carry

    lax.fori_loop(1, NZ, greet_z, 0)
    lax.fori_loop(1, NXY, greet_xy, 0)
    pl.semaphore_signal(barrier, 1, device_id=other, device_id_type=MESH)

    for copy in inputs[:3]:
        copy.wait()
    ids = ids_ref[...]
    owner = jnp.floor((ids.astype(F32) + 0.5) * (1.0 / MOV)).astype(jnp.int32)
    column = rat_ref[...] * PAD + (ids - owner * MOV) + 1
    high = lax.shift_right_logical(column, 5).astype(F32)
    low = (column & 31).astype(F32)
    owner = jnp.where(val_ref[...] == 1, owner, -1)
    row = lax.broadcasted_iota(jnp.int32, (128, 128), 0)
    lane = lax.broadcasted_iota(jnp.int32, (128, 128), 1)
    before = jnp.where(row < lane, 1.0, 0.0).astype(BF16)
    rank_row = (row & 15).astype(F32)
    user_row = lax.shift_right_logical(row, 4) & 3
    hot = [jnp.where(owner[u : u + 1] == row, 1.0, 0.0) for u in range(4)]
    counts = dot(jnp.concatenate(hot, axis=0).astype(BF16), before, 1, 0)
    picks = []
    for u in range(4):
        rank = jnp.sum(hot[u] * counts[u * 128 : (u + 1) * 128], axis=0, keepdims=True)
        part = jnp.where(row < 64, high[u : u + 1], low[u : u + 1])
        picks.append(jnp.where((user_row == u) & (rank_row == rank), part, 0.0))
    table = dot(
        jnp.concatenate(hot, axis=1).astype(BF16), jnp.concatenate(picks, axis=1).astype(BF16), 1, 1
    )
    for i in range(NZ):
        for k in range(NXY):
            t_send[i, k] = table[i * NXY + k : i * NXY + k + 1]

    pl.semaphore_wait(barrier, NZ - 1 + NXY - 1 + 1)

    to_z = z_copies(
        lambda t: t_send.at[t], lambda d: d1.at[z], dz_s.at[0], dz_r.at[0], t_send.at[0 : NZ - 1]
    )
    start(to_z)
    d1[z] = t_send[z]
    for copy in inputs[3:]:
        copy.wait()
    for k in range(LEVELS):
        w_sc[k * PAD + 128 : (k + 1) * PAD] = jnp.zeros((PAD - 128, F), BF16)
        w_sc[k * PAD : k * PAD + MOV] = w_ref[k]
    vb_pad[...] = jnp.zeros((8, 256), F32)
    vb_pad[0:LEVELS, 0:MOV] = vb_ref[...]
    bias_columns = jnp.transpose(vb_pad[...])
    for k in range(LEVELS):
        vbc[k * PAD : (k + 1) * PAD] = jnp.broadcast_to(bias_columns[0:PAD, k : k + 1], (PAD, 128))

    arrived(to_z)
    to_xy = xy_copies(
        lambda t: d1.at[:, t], lambda d: d2.at[xy], dx_s.at[0], dx_r.at[0], d2.at[0 : NXY - 1]
    )
    start(to_xy)
    d2[xy] = d1[:, xy]
    arrived(to_xy)

    for i in range(NXY):
        for k in range(NZ):
            t2d[i * NZ + k : i * NZ + k + 1] = d2[i, k]
    got = jnp.transpose(t2d[...])
    chosen = got[0:64] * 32.0 + got[64:128] - 1.0

    def layout(g):
        first, users, ring_first = GROUPS[g]
        return first // 8, users // 128, ring_first

    def piece(t, g, first_stage):
        base, n, ring_first = layout(g)
        return pl.ds(base + t * n * (2 if ring_first and first_stage else 1), n * (2 if ring_first and first_stage else 1))

    def own_blocks(g):
        return piece(z if layout(g)[2] else xy, g, True)

    def own_chunk(g):
        return lax.rem(xy, NZ) if layout(g)[2] else z

    def own_piece(c, g):
        base, n, ring_first = layout(g)
        blocks = pl.ds(base + (z * 2 + xy // NZ) * n, n) if ring_first else own_blocks(g)
        return hid.at[c, blocks, :, pl.ds(pl.multiple_of(own_chunk(g) * 128, 128), 128)]

    def stage(c, half, g, is_wide, src, dst):
        k, ring = 2 * c + half, layout(g)[2] == is_wide
        base, n, _ = layout(g)
        count = (NZ if ring else NXY) - 1
        rows = n * (2 if layout(g)[2] else 1)
        whole = p_sc.at[c, pl.ds(base, count * rows)] if is_wide else q_sc.at[c, g, 0:count, 0:n]
        if ring:
            return z_copies(src, dst, cz_s.at[k, g], cz_r.at[k, g], whole)
        return xy_copies(src, dst, cx_s.at[k, g], cx_r.at[k, g], whole)

    @functools.cache
    def rs_wide(c, g):
        return stage(c, 0, g, True, lambda t: p_sc.at[c, piece(t, g, True)], lambda d: r1.at[c, piece(d, g, True)])

    @functools.cache
    def rs_narrow(c, g):
        n = layout(g)[1]
        return stage(c, 0, g, False, lambda t: q_sc.at[c, g, t, 0:n], lambda d: r2.at[c, g, d, 0:n])

    @functools.cache
    def ag_narrow(c, g):
        return stage(c, 1, g, False, lambda t: own_piece(c, g), lambda d: own_piece(c, g))

    @functools.cache
    def ag_wide(c, g):
        return stage(c, 1, g, True, lambda t: hid.at[c, own_blocks(g)], lambda d: hid.at[c, own_blocks(g)])

    shared = []

    def share(mine, theirs):
        i = len(shared)
        copy = pltpu.make_async_remote_copy(
            mine, mine, co_s.at[i], co_r.at[i], device_id=other, device_id_type=MESH
        )
        copy.start()
        shared.append(
            pltpu.make_async_remote_copy(
                theirs, theirs, co_s.at[i], co_r.at[i], device_id=other, device_id_type=MESH
            )
        )

    seen = []

    def have_shared(upto):
        for copy in shared[len(seen) : upto]:
            copy.wait_recv()
            seen.append(copy)

    def users_of(g):
        first, users, _ = GROUPS[g]
        return slice(first, first + users)

    def blocks_of(g):
        first, users, _ = GROUPS[g]
        return slice(first // 8, (first + users) // 8)

    def batch_users(b):
        return slice(users_of(b[0]).start, users_of(b[-1]).stop)

    def partial_inputs(c, b, visible):
        sums = dot(visible, w_sc[...], 0, 0)
        first = batch_users(b).start // 8
        p_sc[c, first : first + sums.shape[0] // 8] = sums.reshape(sums.shape[0] // 8, 8, F).astype(BF16)
        for g in b:
            start(rs_wide(c, g))

    def first_sum(c, g):
        arrived(rs_wide(c, g))
        n, ring_first = layout(g)[1:]
        for h in range(2 if ring_first else 1):
            for f in range(NZ):
                cut = slice(f * 128, (f + 1) * 128)
                base = layout(g)[0]
                mine = base + (z * 2 * n if ring_first else xy * n) + h * n
                total = p_sc[c, pl.ds(mine, n), :, cut].astype(F32)
                for d in range(1, NZ if ring_first else NXY):
                    slot = base + d * n * (2 if ring_first else 1) + h * n
                    total = total + r1[c, slot : slot + n, :, cut].astype(F32)
                q_sc[c, g, h * NZ + f, 0:n] = total.astype(BF16)
        start(rs_narrow(c, g))

    def second_sum(c, g):
        arrived(rs_narrow(c, g))
        n, ring_first = layout(g)[1:]
        total = q_sc[c, g, xy if ring_first else z, 0:n].astype(F32)
        for d in range(1, NXY if ring_first else NZ):
            total = total + r2[c, g, d, 0:n].astype(F32)
        value = 1.0 / (1.0 + jnp.exp(-(total + hb_ref[own_chunk(g)])))
        own_piece(c, g)[...] = value.astype(BF16)
        start(ag_narrow(c, g))
        return value

    def gather(c, g):
        arrived(ag_narrow(c, g))
        start(ag_wide(c, g))

    def gathered(c, g):
        arrived(ag_wide(c, g))
        rows = hid[c, blocks_of(g)].astype(F32)
        flat[c, core, users_of(g)] = rows.reshape(rows.shape[0] * 8, F).astype(BF16)
        share(flat.at[c, core, users_of(g)], flat.at[c, 1 - core, users_of(g)])

    for b in BATCHES:
        for u in range(batch_users(b).start // 128, batch_users(b).stop // 128):
            picks = [chosen[u * 16 + k : u * 16 + k + 1] for k in range(CAP)]

            def block(b, carry, picks=picks, u=u):
                base = pl.multiple_of(b * 48, 48)
                at = (lax.broadcasted_iota(jnp.int32, (48, 128), 0) + base).astype(F32)
                hit = picks[0] == at
                for p in picks[1:]:
                    hit = hit | (p == at)
                s_sc[core, pl.ds(base, 48), u * 128 : (u + 1) * 128] = jnp.where(hit, 1.0, 0.0).astype(BF16)
                return carry

            lax.fori_loop(0, COLS // 48, block, 0)
        partial_inputs(0, b, s_sc[core, :, batch_users(b)])
        share(s_sc.at[core, :, batch_users(b)], s_sc.at[1 - core, :, batch_users(b)])
    for step, g in PIPE:
        if step == 0:
            first_sum(0, g)
        elif step == 1:
            pos_own[g, 0 : layout(g)[1]] = second_sum(0, g)
        else:
            gather(0, g)
    for b in BATCHES:
        for g in b:
            gathered(0, g)
        first = batch_users(b).start
        users = batch_users(b).stop - first
        l_sc[:, 0:users] = dot(w_sc[...], flat[0, core, batch_users(b)], 1, 1)

        def softmax(i, carry, first=first, users=users):
            base = pl.multiple_of(i * 16, 16)
            for h in range(users // 128):
                lanes = slice(h * 128, (h + 1) * 128)
                out_lanes = slice(first + h * 128, first + (h + 1) * 128)
                at = [pl.ds(pl.multiple_of(k * PAD + base, 16), 16) for k in range(LEVELS)]
                logits = [l_sc[a, lanes] + vbc[a, :] for a in at]
                largest = functools.reduce(jnp.maximum, logits)
                powers = [jnp.exp(v - largest) for v in logits]
                whole = functools.reduce(jnp.add, powers)
                rated = functools.reduce(jnp.add, [s_sc[core, a, out_lanes].astype(F32) for a in at])
                scale = rated / whole
                for a, v in zip(at, powers):
                    r_sc[core, a, out_lanes] = (v * scale).astype(BF16)
            return carry

        lax.fori_loop(0, PAD // 16, softmax, 0)
        partial_inputs(1, b, r_sc[core, :, batch_users(b)])
        share(r_sc.at[core, :, batch_users(b)], r_sc.at[1 - core, :, batch_users(b)])

    def columns(n):
        return slice(n * 256, (n + 1) * 256)

    for g in SUM_ORDER:
        first_sum(1, g)

    have_shared(len(shared))
    for n in range(F // 256):
        acc_sc[:, columns(n)] = dot(s_sc[0], flat[0, 0, :, columns(n)], 1, 0)
    change = [jnp.zeros((1, 128), F32), jnp.zeros((1, 128), F32)]
    for g in SUM_ORDER:
        value = second_sum(1, g)
        kind = 1 if layout(g)[2] else 0
        moved = jnp.sum(pos_own[g, 0 : layout(g)[1]] - value, axis=0)
        change[kind] = change[kind] + jnp.sum(moved, axis=0, keepdims=True)
    hz[z] = jnp.concatenate(change, axis=0)
    h_z = z_copies(lambda t: hz.at[z], lambda d: hz.at[z], hz_s.at[0], hz_r.at[0], hz.at[0 : NZ - 1])
    start(h_z)
    for n in range(F // 256):
        acc_sc[:, columns(n)] = acc_sc[:, columns(n)] + dot(s_sc[1], flat[0, 1, :, columns(n)], 1, 0)
    for g in SUM_ORDER:
        gather(1, g)
    ones = jnp.ones((8, USERS), BF16)
    for k in range(LEVELS):
        level = slice(k * PAD, (k + 1) * PAD)
        moved = [dot(ones, s_sc[h, level], 1, 1) - dot(ones, r_sc[h, level], 1, 1) for h in range(2)]
        vg_ref[k : k + 1] = (moved[0] + moved[1])[0:1]
    for u in range(4):
        block_rows = hid[0, u * 16 + xy].astype(F32)
        mine = lax.broadcasted_iota(jnp.int32, (8, F), 0) == z
        ph_ref[u : u + 1] = jnp.sum(jnp.where(mine, block_rows, 0.0), axis=0, keepdims=True)

    arrived(h_z)
    rest = functools.reduce(jnp.add, [hz[k, 1:2] for k in range(NZ)])
    for k in range(NZ):
        hxy[xy, k] = hz[k, 0:1] + jnp.where(lax.rem(xy, NZ) == k, rest, 0.0)
    h_xy = xy_copies(
        lambda t: hxy.at[xy], lambda d: hxy.at[xy], hx_s.at[0], hx_r.at[0], hxy.at[0 : NXY - 1]
    )
    start(h_xy)
    upto = []
    for b in BATCHES:
        for g in b:
            gathered(1, g)
        upto.append(len(shared))
    arrived(h_xy)
    total = hxy[0]
    for d in range(1, NXY):
        total = total + hxy[d]
    hco[0] = total
    hg_copy = pltpu.make_async_remote_copy(
        hco.at[0], hco.at[1], hc_s.at[0], hc_r.at[0], device_id=other, device_id_type=MESH
    )
    hg_copy.start()
    for b, last in zip(BATCHES, upto):
        have_shared(last)
        users = batch_users(b)
        for n in range(F // 256):
            moved = dot(r_sc[0, :, users], flat[1, 0, users, columns(n)], 1, 0) + dot(
                r_sc[1, :, users], flat[1, 1, users, columns(n)], 1, 0
            )
            total = acc_sc[:, columns(n)] - moved
            if b != BATCHES[-1]:
                acc_sc[:, columns(n)] = total
                continue
            for k in range(LEVELS):
                wg_ref[k, :, columns(n)] = total[k * PAD : k * PAD + MOV]
    hg_copy.wait_recv()
    for copies in started:
        sent(copies)
    for copy in (hg_copy, *shared):
        copy.wait_send()


def finish(wg_ref, vg_ref, hco_ref, ph_ref, wg_out, vg_out, hg_out, ph_out, vg, hg, sem):
    copies = [
        pltpu.make_async_copy(src, dst, sem.at[i])
        for i, (src, dst) in enumerate(((wg_ref, wg_out), (ph_ref, ph_out), (vg, vg_out), (hg, hg_out)))
    ]
    copies[0].start()
    copies[1].start()
    vg[...] = vg_ref[0:LEVELS, 0:MOV]
    copies[2].start()
    hg[...] = hco_ref[0] + hco_ref[1]
    copies[3].start()
    for copy in copies:
        copy.wait()


def on_device(movie_ids, ratings, valid, weights, vis_bias, hid_bias):
    dma = pltpu.SemaphoreType.DMA
    vmem = pl.BlockSpec(memory_space=pltpu.VMEM)
    hbm = pl.BlockSpec(memory_space=pltpu.HBM)
    shape = jax.ShapeDtypeStruct
    parts = pl.pallas_call(
        kernel,
        out_shape=(
            shape((LEVELS, MOV, F), F32),
            shape((8, PAD), F32),
            shape((2, NZ, 1, 128), F32),
            shape((4, F), F32),
        ),
        in_specs=[hbm] * 6,
        out_specs=(vmem,) * 4,
        scratch_shapes=[
            pltpu.VMEM((4, 128), jnp.int32), pltpu.VMEM((4, 128), jnp.int32), pltpu.VMEM((4, 128), jnp.int32),
            pltpu.VMEM((LEVELS, MOV, F), BF16), pltpu.VMEM((LEVELS, MOV), F32), pltpu.VMEM((NZ, 1, 128), F32),
            dma((6,)),
            pltpu.VMEM((COLS, F), BF16),
            pltpu.VMEM((8, 256), F32),
            pltpu.VMEM((COLS, 128), F32),
            pltpu.VMEM((128, 128), F32),
            pltpu.VMEM((NZ, NXY, 1, 128), F32),
            pltpu.VMEM((NZ, NXY, 1, 128), F32),
            pltpu.VMEM((NXY, NZ, 1, 128), F32),
            pltpu.VMEM((2, COLS, USERS), BF16),
            pltpu.VMEM((2, COLS, USERS), BF16),
            pltpu.VMEM((COLS, WIDEST), F32),
            pltpu.VMEM((2, BLOCKS, 8, F), BF16),
            pltpu.VMEM((2, BLOCKS, 8, F), BF16),
            pltpu.VMEM((2, len(GROUPS), NXY, MOST // 128, 8, 128), BF16),
            pltpu.VMEM((2, len(GROUPS), NXY, MOST // 128, 8, 128), BF16),
            pltpu.VMEM((2, BLOCKS, 8, F), BF16),
            pltpu.VMEM((2, 2, USERS, F), BF16),
            pltpu.VMEM((len(GROUPS), MOST // 128, 8, 128), F32),
            pltpu.VMEM((COLS, F), F32),
            pltpu.VMEM((NZ, 2, 128), F32),
            pltpu.VMEM((NXY, NZ, 1, 128), F32),
            *[dma((1,))] * 4, *[dma((4, len(GROUPS)))] * 4, *[dma((1,))] * 4,
            dma((1,)), dma((1,)), dma((2 * len(BATCHES) + 2 * len(GROUPS),)), dma((2 * len(BATCHES) + 2 * len(GROUPS),)),
        ],
        compiler_params=pltpu.CompilerParams(
            collective_id=0, has_side_effects=True, vmem_limit_bytes=36 << 20
        ),
    )(*[
        pltpu.with_memory_space_constraint(a, pltpu.HBM)
        for a in (movie_ids, ratings, valid, weights, vis_bias, hid_bias.reshape(NZ, 1, 128))
    ])
    wg, vg, hg, ph = pl.pallas_call(
        finish,
        out_shape=(shape((LEVELS, MOV, F), F32), shape((LEVELS, MOV), F32), shape((NZ, 1, 128), F32), shape((4, F), F32)),
        in_specs=[vmem] * 4,
        out_specs=(hbm,) * 4,
        scratch_shapes=[
            pltpu.VMEM((LEVELS, MOV), F32), pltpu.VMEM((NZ, 1, 128), F32), dma((4,)),
        ],
        compiler_params=pltpu.CompilerParams(vmem_limit_bytes=8 << 20),
    )(*parts)
    return wg, vg, hg.reshape(F), ph


def solution(mesh):
    split = Mesh(mesh.devices.reshape(NZ, 4, 4, mesh.shape["user"]), ALL)
    owner = ("z", "y", "x")
    in_specs = (P(ALL, None), P(ALL, None), P(ALL, None), P(None, owner, None), P(None, owner), P())
    out_specs = (P(None, owner, None), P(None, owner), P(), P(ALL, None))
    return jax.shard_map(on_device, mesh=split, in_specs=in_specs, out_specs=out_specs, check_vma=False)
```

```python
import functools

import jax
import jax.numpy as jnp
from jax import lax
from jax.experimental import pallas as pl
from jax.experimental.pallas import tpu as pltpu
from jax.sharding import Mesh
from jax.sharding import PartitionSpec as P

LEVELS = 5
MOV = 140
PAD = 144
COLS = LEVELS * PAD
F = 1024
NZ, NXY = 8, 16
CAP = 12
USERS = 512
BLOCKS = USERS // 8
GROUPS = ((0, 128, True), (128, 128, False), (256, 128, False), (384, 128, False))
SUM_ORDER = (0, 1, 2, 3)
PIPE = ((0, 1), (0, 0), (0, 2), (1, 1), (0, 3), (1, 0), (1, 2), (2, 1), (1, 3), (2, 0), (2, 2), (2, 3))
BATCHES = ((0, 1), (2, 3))
MOST = max(n for _, n, _ in GROUPS)
WIDEST = 256
ALL = ("z", "y", "x", "core")
MESH = pl.DeviceIdType.MESH
F32, BF16 = jnp.float32, jnp.bfloat16


def dot(a, b, ca, cb):
    return lax.dot_general(a, b, (((ca,), (cb,)), ((), ())), preferred_element_type=F32)


def kernel(
    ids_hbm, rat_hbm, val_hbm, w_hbm, vb_hbm, hb_hbm,
    wg_ref, vg_ref, hco, ph_ref,
    ids_ref, rat_ref, val_ref, w_ref, vb_ref, hb_ref, in_sem,
    w_sc, vb_pad, vbc, t2d, t_send, d1, d2, s_sc, r_sc, l_sc,
    p_sc, r1, q_sc, r2, hid, flat, pos_own, acc_sc, hz, hxy,
    dz_s, dz_r, dx_s, dx_r, cz_s, cz_r, cx_s, cx_r, hz_s, hz_r, hx_s, hx_r, hc_s, hc_r, co_s, co_r,
):
    z, y, x, core = [lax.axis_index(a) for a in ALL]
    xy = y * 4 + x
    other = (z, y, x, 1 - core)

    def xy_peer(d):
        return lax.rem(y + d // 4, 4), lax.rem(x + lax.rem(d, 4), 4)

    def z_peer(d):
        return lax.rem(z + d, NZ)

    def xy_copies(src, dst, send, recv, whole):
        def copy(d):
            ty, tx = xy_peer(d)
            return pltpu.make_async_remote_copy(
                src(ty * 4 + tx), dst(d), send, recv, device_id=(z, ty, tx, core), device_id_type=MESH
            )

        return NXY, copy, send, recv, whole

    def z_copies(src, dst, send, recv, whole):
        def copy(d):
            tz = z_peer(d)
            return pltpu.make_async_remote_copy(
                src(tz), dst(d), send, recv, device_id=(tz, y, x, core), device_id_type=MESH
            )

        return NZ, copy, send, recv, whole

    started = []

    def start(copies):
        started.append(copies)
        n, copy = copies[:2]

        def step(d, carry):
            copy(d).start()
            return carry

        lax.fori_loop(1, n, step, 0)

    def all_of(copies):
        send, recv, whole = copies[2:]
        return pltpu.make_async_remote_copy(whole, whole, send, recv, device_id=other, device_id_type=MESH)

    def arrived(copies):
        all_of(copies).wait_recv()

    def sent(copies):
        all_of(copies).wait_send()

    inputs = [
        pltpu.make_async_copy(src, dst, in_sem.at[i])
        for i, (src, dst) in enumerate(
            (
                (ids_hbm, ids_ref), (rat_hbm, rat_ref), (val_hbm, val_ref),
                (w_hbm, w_ref), (vb_hbm, vb_ref), (hb_hbm, hb_ref),
            )
        )
    ]
    for copy in inputs:
        copy.start()

    barrier = pltpu.get_barrier_semaphore()

    def greet_xy(d, carry):
        ty, tx = xy_peer(d)
        pl.semaphore_signal(barrier, 1, device_id=(z, ty, tx, core), device_id_type=MESH)
        return carry

    def greet_z(d, carry):
        pl.semaphore_signal(barrier, 1, device_id=(z_peer(d), y, x, core), device_id_type=MESH)
        return carry

    lax.fori_loop(1, NZ, greet_z, 0)
    lax.fori_loop(1, NXY, greet_xy, 0)
    pl.semaphore_signal(barrier, 1, device_id=other, device_id_type=MESH)

    for copy in inputs[:3]:
        copy.wait()
    ids = ids_ref[...]
    owner = jnp.floor((ids.astype(F32) + 0.5) * (1.0 / MOV)).astype(jnp.int32)
    column = rat_ref[...] * PAD + (ids - owner * MOV) + 1
    high = lax.shift_right_logical(column, 5).astype(F32)
    low = (column & 31).astype(F32)
    owner = jnp.where(val_ref[...] == 1, owner, -1)
    row = lax.broadcasted_iota(jnp.int32, (128, 128), 0)
    lane = lax.broadcasted_iota(jnp.int32, (128, 128), 1)
    before = jnp.where(row < lane, 1.0, 0.0).astype(BF16)
    rank_row = (row & 15).astype(F32)
    user_row = lax.shift_right_logical(row, 4) & 3
    hot = [jnp.where(owner[u : u + 1] == row, 1.0, 0.0) for u in range(4)]
    counts = dot(jnp.concatenate(hot, axis=0).astype(BF16), before, 1, 0)
    picks = []
    for u in range(4):
        rank = jnp.sum(hot[u] * counts[u * 128 : (u + 1) * 128], axis=0, keepdims=True)
        part = jnp.where(row < 64, high[u : u + 1], low[u : u + 1])
        picks.append(jnp.where((user_row == u) & (rank_row == rank), part, 0.0))
    table = dot(
        jnp.concatenate(hot, axis=1).astype(BF16), jnp.concatenate(picks, axis=1).astype(BF16), 1, 1
    )
    for i in range(NZ):
        for k in range(NXY):
            t_send[i, k] = table[i * NXY + k : i * NXY + k + 1]

    pl.semaphore_wait(barrier, NZ - 1 + NXY - 1 + 1)

    to_z = z_copies(
        lambda t: t_send.at[t], lambda d: d1.at[z], dz_s.at[0], dz_r.at[0], t_send.at[0 : NZ - 1]
    )
    start(to_z)
    d1[z] = t_send[z]
    for copy in inputs[3:]:
        copy.wait()
    for k in range(LEVELS):
        w_sc[k * PAD + 128 : (k + 1) * PAD] = jnp.zeros((PAD - 128, F), BF16)
        w_sc[k * PAD : k * PAD + MOV] = w_ref[k]
    vb_pad[...] = jnp.zeros((8, 256), F32)
    vb_pad[0:LEVELS, 0:MOV] = vb_ref[...]
    bias_columns = jnp.transpose(vb_pad[...])
    for k in range(LEVELS):
        vbc[k * PAD : (k + 1) * PAD] = jnp.broadcast_to(bias_columns[0:PAD, k : k + 1], (PAD, 128))

    arrived(to_z)
    to_xy = xy_copies(
        lambda t: d1.at[:, t], lambda d: d2.at[xy], dx_s.at[0], dx_r.at[0], d2.at[0 : NXY - 1]
    )
    start(to_xy)
    d2[xy] = d1[:, xy]
    arrived(to_xy)

    for i in range(NXY):
        for k in range(NZ):
            t2d[i * NZ + k : i * NZ + k + 1] = d2[i, k]
    got = jnp.transpose(t2d[...])
    chosen = got[0:64] * 32.0 + got[64:128] - 1.0

    def layout(g):
        first, users, ring_first = GROUPS[g]
        return first // 8, users // 128, ring_first

    def piece(t, g, first_stage):
        base, n, ring_first = layout(g)
        return pl.ds(base + t * n * (2 if ring_first and first_stage else 1), n * (2 if ring_first and first_stage else 1))

    def own_blocks(g):
        return piece(z if layout(g)[2] else xy, g, True)

    def own_chunk(g):
        return lax.rem(xy, NZ) if layout(g)[2] else z

    def own_piece(c, g):
        base, n, ring_first = layout(g)
        blocks = pl.ds(base + (z * 2 + xy // NZ) * n, n) if ring_first else own_blocks(g)
        return hid.at[c, blocks, :, pl.ds(pl.multiple_of(own_chunk(g) * 128, 128), 128)]

    def stage(c, half, g, is_wide, src, dst):
        k, ring = 2 * c + half, layout(g)[2] == is_wide
        base, n, _ = layout(g)
        count = (NZ if ring else NXY) - 1
        rows = n * (2 if layout(g)[2] else 1)
        whole = p_sc.at[c, pl.ds(base, count * rows)] if is_wide else q_sc.at[c, g, 0:count, 0:n]
        if ring:
            return z_copies(src, dst, cz_s.at[k, g], cz_r.at[k, g], whole)
        return xy_copies(src, dst, cx_s.at[k, g], cx_r.at[k, g], whole)

    @functools.cache
    def rs_wide(c, g):
        return stage(c, 0, g, True, lambda t: p_sc.at[c, piece(t, g, True)], lambda d: r1.at[c, piece(d, g, True)])

    @functools.cache
    def rs_narrow(c, g):
        n = layout(g)[1]
        return stage(c, 0, g, False, lambda t: q_sc.at[c, g, t, 0:n], lambda d: r2.at[c, g, d, 0:n])

    @functools.cache
    def ag_narrow(c, g):
        return stage(c, 1, g, False, lambda t: own_piece(c, g), lambda d: own_piece(c, g))

    @functools.cache
    def ag_wide(c, g):
        return stage(c, 1, g, True, lambda t: hid.at[c, own_blocks(g)], lambda d: hid.at[c, own_blocks(g)])

    shared = []

    def share(mine, theirs):
        i = len(shared)
        copy = pltpu.make_async_remote_copy(
            mine, mine, co_s.at[i], co_r.at[i], device_id=other, device_id_type=MESH
        )
        copy.start()
        shared.append(
            pltpu.make_async_remote_copy(
                theirs, theirs, co_s.at[i], co_r.at[i], device_id=other, device_id_type=MESH
            )
        )

    seen = []

    def have_shared(upto):
        for copy in shared[len(seen) : upto]:
            copy.wait_recv()
            seen.append(copy)

    def users_of(g):
        first, users, _ = GROUPS[g]
        return slice(first, first + users)

    def blocks_of(g):
        first, users, _ = GROUPS[g]
        return slice(first // 8, (first + users) // 8)

    def batch_users(b):
        return slice(users_of(b[0]).start, users_of(b[-1]).stop)

    def partial_inputs(c, b, visible):
        sums = dot(visible, w_sc[...], 0, 0)
        first = batch_users(b).start // 8
        p_sc[c, first : first + sums.shape[0] // 8] = sums.reshape(sums.shape[0] // 8, 8, F).astype(BF16)
        for g in b:
            start(rs_wide(c, g))

    def first_sum(c, g):
        arrived(rs_wide(c, g))
        n, ring_first = layout(g)[1:]
        for h in range(2 if ring_first else 1):
            for f in range(NZ):
                cut = slice(f * 128, (f + 1) * 128)
                base = layout(g)[0]
                mine = base + (z * 2 * n if ring_first else xy * n) + h * n
                total = p_sc[c, pl.ds(mine, n), :, cut].astype(F32)
                for d in range(1, NZ if ring_first else NXY):
                    slot = base + d * n * (2 if ring_first else 1) + h * n
                    total = total + r1[c, slot : slot + n, :, cut].astype(F32)
                q_sc[c, g, h * NZ + f, 0:n] = total.astype(BF16)
        start(rs_narrow(c, g))

    def second_sum(c, g):
        arrived(rs_narrow(c, g))
        n, ring_first = layout(g)[1:]
        total = q_sc[c, g, xy if ring_first else z, 0:n].astype(F32)
        for d in range(1, NXY if ring_first else NZ):
            total = total + r2[c, g, d, 0:n].astype(F32)
        value = 1.0 / (1.0 + jnp.exp(-(total + hb_ref[own_chunk(g)])))
        own_piece(c, g)[...] = value.astype(BF16)
        start(ag_narrow(c, g))
        return value

    def gather(c, g):
        arrived(ag_narrow(c, g))
        start(ag_wide(c, g))

    def gathered(c, g):
        arrived(ag_wide(c, g))
        rows = hid[c, blocks_of(g)].astype(F32)
        flat[c, core, users_of(g)] = rows.reshape(rows.shape[0] * 8, F).astype(BF16)
        share(flat.at[c, core, users_of(g)], flat.at[c, 1 - core, users_of(g)])

    for b in ((0,), (1,), (2, 3)):
        for u in range(batch_users(b).start // 128, batch_users(b).stop // 128):
            picks = [chosen[u * 16 + k : u * 16 + k + 1] for k in range(CAP)]

            def block(b, carry, picks=picks, u=u):
                base = pl.multiple_of(b * 48, 48)
                at = (lax.broadcasted_iota(jnp.int32, (48, 128), 0) + base).astype(F32)
                hit = picks[0] == at
                for p in picks[1:]:
                    hit = hit | (p == at)
                s_sc[core, pl.ds(base, 48), u * 128 : (u + 1) * 128] = jnp.where(hit, 1.0, 0.0).astype(BF16)
                return carry

            lax.fori_loop(0, COLS // 48, block, 0)
        partial_inputs(0, b, s_sc[core, :, batch_users(b)])
        share(s_sc.at[core, :, batch_users(b)], s_sc.at[1 - core, :, batch_users(b)])
    for step, g in PIPE:
        if step == 0:
            first_sum(0, g)
        elif step == 1:
            pos_own[g, 0 : layout(g)[1]] = second_sum(0, g)
        else:
            gather(0, g)
    for b in BATCHES:
        for g in b:
            gathered(0, g)
        first = batch_users(b).start
        users = batch_users(b).stop - first
        l_sc[:, 0:users] = dot(w_sc[...], flat[0, core, batch_users(b)], 1, 1)

        def softmax(i, carry, first=first, users=users):
            base = pl.multiple_of(i * 16, 16)
            for h in range(users // 128):
                lanes = slice(h * 128, (h + 1) * 128)
                out_lanes = slice(first + h * 128, first + (h + 1) * 128)
                at = [pl.ds(pl.multiple_of(k * PAD + base, 16), 16) for k in range(LEVELS)]
                logits = [l_sc[a, lanes] + vbc[a, :] for a in at]
                largest = functools.reduce(jnp.maximum, logits)
                powers = [jnp.exp(v - largest) for v in logits]
                whole = functools.reduce(jnp.add, powers)
                rated = functools.reduce(jnp.add, [s_sc[core, a, out_lanes].astype(F32) for a in at])
                scale = rated / whole
                for a, v in zip(at, powers):
                    r_sc[core, a, out_lanes] = (v * scale).astype(BF16)
            return carry

        lax.fori_loop(0, PAD // 16, softmax, 0)
        partial_inputs(1, b, r_sc[core, :, batch_users(b)])
        share(r_sc.at[core, :, batch_users(b)], r_sc.at[1 - core, :, batch_users(b)])

    def columns(n):
        return slice(n * 256, (n + 1) * 256)

    for g in SUM_ORDER:
        first_sum(1, g)

    have_shared(len(shared))
    for n in range(F // 256):
        acc_sc[:, columns(n)] = dot(s_sc[0], flat[0, 0, :, columns(n)], 1, 0)
    change = [jnp.zeros((1, 128), F32), jnp.zeros((1, 128), F32)]
    for g in SUM_ORDER:
        value = second_sum(1, g)
        kind = 1 if layout(g)[2] else 0
        moved = jnp.sum(pos_own[g, 0 : layout(g)[1]] - value, axis=0)
        change[kind] = change[kind] + jnp.sum(moved, axis=0, keepdims=True)
    hz[z] = jnp.concatenate(change, axis=0)
    h_z = z_copies(lambda t: hz.at[z], lambda d: hz.at[z], hz_s.at[0], hz_r.at[0], hz.at[0 : NZ - 1])
    start(h_z)
    for n in range(F // 256):
        acc_sc[:, columns(n)] = acc_sc[:, columns(n)] + dot(s_sc[1], flat[0, 1, :, columns(n)], 1, 0)
    for g in SUM_ORDER:
        gather(1, g)
    ones = jnp.ones((8, USERS), BF16)
    for k in range(LEVELS):
        level = slice(k * PAD, (k + 1) * PAD)
        moved = [dot(ones, s_sc[h, level], 1, 1) - dot(ones, r_sc[h, level], 1, 1) for h in range(2)]
        vg_ref[k : k + 1] = (moved[0] + moved[1])[0:1]
    for u in range(4):
        block_rows = hid[0, u * 16 + xy].astype(F32)
        mine = lax.broadcasted_iota(jnp.int32, (8, F), 0) == z
        ph_ref[u : u + 1] = jnp.sum(jnp.where(mine, block_rows, 0.0), axis=0, keepdims=True)

    arrived(h_z)
    rest = functools.reduce(jnp.add, [hz[k, 1:2] for k in range(NZ)])
    for k in range(NZ):
        hxy[xy, k] = hz[k, 0:1] + jnp.where(lax.rem(xy, NZ) == k, rest, 0.0)
    h_xy = xy_copies(
        lambda t: hxy.at[xy], lambda d: hxy.at[xy], hx_s.at[0], hx_r.at[0], hxy.at[0 : NXY - 1]
    )
    start(h_xy)
    upto = []
    for b in BATCHES:
        for g in b:
            gathered(1, g)
        upto.append(len(shared))
    arrived(h_xy)
    total = hxy[0]
    for d in range(1, NXY):
        total = total + hxy[d]
    hco[0] = total
    hg_copy = pltpu.make_async_remote_copy(
        hco.at[0], hco.at[1], hc_s.at[0], hc_r.at[0], device_id=other, device_id_type=MESH
    )
    hg_copy.start()
    for b, last in zip(BATCHES, upto):
        have_shared(last)
        users = batch_users(b)
        for n in range(F // 256):
            moved = dot(r_sc[0, :, users], flat[1, 0, users, columns(n)], 1, 0) + dot(
                r_sc[1, :, users], flat[1, 1, users, columns(n)], 1, 0
            )
            total = acc_sc[:, columns(n)] - moved
            if b != BATCHES[-1]:
                acc_sc[:, columns(n)] = total
                continue
            for k in range(LEVELS):
                wg_ref[k, :, columns(n)] = total[k * PAD : k * PAD + MOV]
    hg_copy.wait_recv()
    for copies in started:
        sent(copies)
    for copy in (hg_copy, *shared):
        copy.wait_send()


def finish(wg_ref, vg_ref, hco_ref, ph_ref, wg_out, vg_out, hg_out, ph_out, vg, hg, sem):
    copies = [
        pltpu.make_async_copy(src, dst, sem.at[i])
        for i, (src, dst) in enumerate(((wg_ref, wg_out), (ph_ref, ph_out), (vg, vg_out), (hg, hg_out)))
    ]
    copies[0].start()
    copies[1].start()
    vg[...] = vg_ref[0:LEVELS, 0:MOV]
    copies[2].start()
    hg[...] = hco_ref[0] + hco_ref[1]
    copies[3].start()
    for copy in copies:
        copy.wait()


def on_device(movie_ids, ratings, valid, weights, vis_bias, hid_bias):
    dma = pltpu.SemaphoreType.DMA
    vmem = pl.BlockSpec(memory_space=pltpu.VMEM)
    hbm = pl.BlockSpec(memory_space=pltpu.HBM)
    shape = jax.ShapeDtypeStruct
    parts = pl.pallas_call(
        kernel,
        out_shape=(
            shape((LEVELS, MOV, F), F32),
            shape((8, PAD), F32),
            shape((2, NZ, 1, 128), F32),
            shape((4, F), F32),
        ),
        in_specs=[hbm] * 6,
        out_specs=(vmem,) * 4,
        scratch_shapes=[
            pltpu.VMEM((4, 128), jnp.int32), pltpu.VMEM((4, 128), jnp.int32), pltpu.VMEM((4, 128), jnp.int32),
            pltpu.VMEM((LEVELS, MOV, F), BF16), pltpu.VMEM((LEVELS, MOV), F32), pltpu.VMEM((NZ, 1, 128), F32),
            dma((6,)),
            pltpu.VMEM((COLS, F), BF16),
            pltpu.VMEM((8, 256), F32),
            pltpu.VMEM((COLS, 128), F32),
            pltpu.VMEM((128, 128), F32),
            pltpu.VMEM((NZ, NXY, 1, 128), F32),
            pltpu.VMEM((NZ, NXY, 1, 128), F32),
            pltpu.VMEM((NXY, NZ, 1, 128), F32),
            pltpu.VMEM((2, COLS, USERS), BF16),
            pltpu.VMEM((2, COLS, USERS), BF16),
            pltpu.VMEM((COLS, WIDEST), F32),
            pltpu.VMEM((2, BLOCKS, 8, F), BF16),
            pltpu.VMEM((2, BLOCKS, 8, F), BF16),
            pltpu.VMEM((2, len(GROUPS), NXY, MOST // 128, 8, 128), BF16),
            pltpu.VMEM((2, len(GROUPS), NXY, MOST // 128, 8, 128), BF16),
            pltpu.VMEM((2, BLOCKS, 8, F), BF16),
            pltpu.VMEM((2, 2, USERS, F), BF16),
            pltpu.VMEM((len(GROUPS), MOST // 128, 8, 128), F32),
            pltpu.VMEM((COLS, F), F32),
            pltpu.VMEM((NZ, 2, 128), F32),
            pltpu.VMEM((NXY, NZ, 1, 128), F32),
            *[dma((1,))] * 4, *[dma((4, len(GROUPS)))] * 4, *[dma((1,))] * 4,
            dma((1,)), dma((1,)), dma((4 * len(GROUPS),)), dma((4 * len(GROUPS),)),
        ],
        compiler_params=pltpu.CompilerParams(
            collective_id=0, has_side_effects=True, vmem_limit_bytes=36 << 20
        ),
    )(*[
        pltpu.with_memory_space_constraint(a, pltpu.HBM)
        for a in (movie_ids, ratings, valid, weights, vis_bias, hid_bias.reshape(NZ, 1, 128))
    ])
    wg, vg, hg, ph = pl.pallas_call(
        finish,
        out_shape=(shape((LEVELS, MOV, F), F32), shape((LEVELS, MOV), F32), shape((NZ, 1, 128), F32), shape((4, F), F32)),
        in_specs=[vmem] * 4,
        out_specs=(hbm,) * 4,
        scratch_shapes=[
            pltpu.VMEM((LEVELS, MOV), F32), pltpu.VMEM((NZ, 1, 128), F32), dma((4,)),
        ],
        compiler_params=pltpu.CompilerParams(vmem_limit_bytes=8 << 20),
    )(*parts)
    return wg, vg, hg.reshape(F), ph


def solution(mesh):
    split = Mesh(mesh.devices.reshape(NZ, 4, 4, mesh.shape["user"]), ALL)
    owner = ("z", "y", "x")
    in_specs = (P(ALL, None), P(ALL, None), P(ALL, None), P(None, owner, None), P(None, owner), P())
    out_specs = (P(None, owner, None), P(None, owner), P(), P(ALL, None))
    return jax.shard_map(on_device, mesh=split, in_specs=in_specs, out_specs=out_specs, check_vma=False)
```

```python
import functools

import jax
import jax.numpy as jnp
from jax import lax
from jax.experimental import pallas as pl
from jax.experimental.pallas import tpu as pltpu
from jax.sharding import Mesh
from jax.sharding import PartitionSpec as P

LEVELS = 5
MOV = 140
PAD = 144
COLS = LEVELS * PAD
F = 1024
NZ, NXY = 8, 16
CAP = 12
USERS = 512
BLOCKS = USERS // 8
GROUPS = ((0, 128, True), (128, 128, False), (256, 128, False), (384, 128, False))
SUM_ORDER = (0, 1, 2, 3)
PIPE = ((0, 1), (0, 0), (0, 2), (0, 3), (1, 1), (1, 0), (1, 2), (2, 1), (1, 3), (2, 0), (2, 2), (2, 3))
BATCHES = ((0, 1), (2, 3))
MOST = max(n for _, n, _ in GROUPS)
WIDEST = 256
ALL = ("z", "y", "x", "core")
MESH = pl.DeviceIdType.MESH
F32, BF16 = jnp.float32, jnp.bfloat16


def dot(a, b, ca, cb):
    return lax.dot_general(a, b, (((ca,), (cb,)), ((), ())), preferred_element_type=F32)


def kernel(
    ids_hbm, rat_hbm, val_hbm, w_hbm, vb_hbm, hb_hbm,
    wg_ref, vg_ref, hco, ph_ref,
    ids_ref, rat_ref, val_ref, w_ref, vb_ref, hb_ref, in_sem,
    w_sc, vb_pad, vbc, t2d, t_send, d1, d2, s_sc, r_sc, l_sc,
    p_sc, r1, q_sc, r2, hid, flat, pos_own, acc_sc, hz, hxy,
    dz_s, dz_r, dx_s, dx_r, cz_s, cz_r, cx_s, cx_r, hz_s, hz_r, hx_s, hx_r, hc_s, hc_r, co_s, co_r,
):
    z, y, x, core = [lax.axis_index(a) for a in ALL]
    xy = y * 4 + x
    other = (z, y, x, 1 - core)

    def xy_peer(d):
        return lax.rem(y + d // 4, 4), lax.rem(x + lax.rem(d, 4), 4)

    def z_peer(d):
        return lax.rem(z + d, NZ)

    def xy_copies(src, dst, send, recv, whole):
        def copy(d):
            ty, tx = xy_peer(d)
            return pltpu.make_async_remote_copy(
                src(ty * 4 + tx), dst(d), send, recv, device_id=(z, ty, tx, core), device_id_type=MESH
            )

        return NXY, copy, send, recv, whole

    def z_copies(src, dst, send, recv, whole):
        def copy(d):
            tz = z_peer(d)
            return pltpu.make_async_remote_copy(
                src(tz), dst(d), send, recv, device_id=(tz, y, x, core), device_id_type=MESH
            )

        return NZ, copy, send, recv, whole

    started = []

    def start(copies):
        started.append(copies)
        n, copy = copies[:2]

        def step(d, carry):
            copy(d).start()
            return carry

        lax.fori_loop(1, n, step, 0)

    def all_of(copies):
        send, recv, whole = copies[2:]
        return pltpu.make_async_remote_copy(whole, whole, send, recv, device_id=other, device_id_type=MESH)

    def arrived(copies):
        all_of(copies).wait_recv()

    def sent(copies):
        all_of(copies).wait_send()

    inputs = [
        pltpu.make_async_copy(src, dst, in_sem.at[i])
        for i, (src, dst) in enumerate(
            (
                (ids_hbm, ids_ref), (rat_hbm, rat_ref), (val_hbm, val_ref),
                (w_hbm, w_ref), (vb_hbm, vb_ref), (hb_hbm, hb_ref),
            )
        )
    ]
    for copy in inputs:
        copy.start()

    barrier = pltpu.get_barrier_semaphore()

    def greet_xy(d, carry):
        ty, tx = xy_peer(d)
        pl.semaphore_signal(barrier, 1, device_id=(z, ty, tx, core), device_id_type=MESH)
        return carry

    def greet_z(d, carry):
        pl.semaphore_signal(barrier, 1, device_id=(z_peer(d), y, x, core), device_id_type=MESH)
        return carry

    lax.fori_loop(1, NZ, greet_z, 0)
    lax.fori_loop(1, NXY, greet_xy, 0)
    pl.semaphore_signal(barrier, 1, device_id=other, device_id_type=MESH)

    for copy in inputs[:3]:
        copy.wait()
    ids = ids_ref[...]
    owner = jnp.floor((ids.astype(F32) + 0.5) * (1.0 / MOV)).astype(jnp.int32)
    column = rat_ref[...] * PAD + (ids - owner * MOV) + 1
    high = lax.shift_right_logical(column, 5).astype(F32)
    low = (column & 31).astype(F32)
    owner = jnp.where(val_ref[...] == 1, owner, -1)
    row = lax.broadcasted_iota(jnp.int32, (128, 128), 0)
    lane = lax.broadcasted_iota(jnp.int32, (128, 128), 1)
    before = jnp.where(row < lane, 1.0, 0.0).astype(BF16)
    rank_row = (row & 15).astype(F32)
    user_row = lax.shift_right_logical(row, 4) & 3
    hot = [jnp.where(owner[u : u + 1] == row, 1.0, 0.0) for u in range(4)]
    counts = dot(jnp.concatenate(hot, axis=0).astype(BF16), before, 1, 0)
    picks = []
    for u in range(4):
        rank = jnp.sum(hot[u] * counts[u * 128 : (u + 1) * 128], axis=0, keepdims=True)
        part = jnp.where(row < 64, high[u : u + 1], low[u : u + 1])
        picks.append(jnp.where((user_row == u) & (rank_row == rank), part, 0.0))
    table = dot(
        jnp.concatenate(hot, axis=1).astype(BF16), jnp.concatenate(picks, axis=1).astype(BF16), 1, 1
    )
    for i in range(NZ):
        for k in range(NXY):
            t_send[i, k] = table[i * NXY + k : i * NXY + k + 1]

    pl.semaphore_wait(barrier, NZ - 1 + NXY - 1 + 1)

    to_z = z_copies(
        lambda t: t_send.at[t], lambda d: d1.at[z], dz_s.at[0], dz_r.at[0], t_send.at[0 : NZ - 1]
    )
    start(to_z)
    d1[z] = t_send[z]
    for copy in inputs[3:]:
        copy.wait()
    for k in range(LEVELS):
        w_sc[k * PAD + 128 : (k + 1) * PAD] = jnp.zeros((PAD - 128, F), BF16)
        w_sc[k * PAD : k * PAD + MOV] = w_ref[k]
    vb_pad[...] = jnp.zeros((8, 256), F32)
    vb_pad[0:LEVELS, 0:MOV] = vb_ref[...]
    bias_columns = jnp.transpose(vb_pad[...])
    for k in range(LEVELS):
        vbc[k * PAD : (k + 1) * PAD] = jnp.broadcast_to(bias_columns[0:PAD, k : k + 1], (PAD, 128))

    arrived(to_z)
    to_xy = xy_copies(
        lambda t: d1.at[:, t], lambda d: d2.at[xy], dx_s.at[0], dx_r.at[0], d2.at[0 : NXY - 1]
    )
    start(to_xy)
    d2[xy] = d1[:, xy]
    arrived(to_xy)

    for i in range(NXY):
        for k in range(NZ):
            t2d[i * NZ + k : i * NZ + k + 1] = d2[i, k]
    got = jnp.transpose(t2d[...])
    chosen = got[0:64] * 32.0 + got[64:128] - 1.0

    def layout(g):
        first, users, ring_first = GROUPS[g]
        return first // 8, users // 128, ring_first

    def piece(t, g, first_stage):
        base, n, ring_first = layout(g)
        return pl.ds(base + t * n * (2 if ring_first and first_stage else 1), n * (2 if ring_first and first_stage else 1))

    def own_blocks(g):
        return piece(z if layout(g)[2] else xy, g, True)

    def own_chunk(g):
        return lax.rem(xy, NZ) if layout(g)[2] else z

    def own_piece(c, g):
        base, n, ring_first = layout(g)
        blocks = pl.ds(base + (z * 2 + xy // NZ) * n, n) if ring_first else own_blocks(g)
        return hid.at[c, blocks, :, pl.ds(pl.multiple_of(own_chunk(g) * 128, 128), 128)]

    def stage(c, half, g, is_wide, src, dst):
        k, ring = 2 * c + half, layout(g)[2] == is_wide
        base, n, _ = layout(g)
        count = (NZ if ring else NXY) - 1
        rows = n * (2 if layout(g)[2] else 1)
        whole = p_sc.at[c, pl.ds(base, count * rows)] if is_wide else q_sc.at[c, g, 0:count, 0:n]
        if ring:
            return z_copies(src, dst, cz_s.at[k, g], cz_r.at[k, g], whole)
        return xy_copies(src, dst, cx_s.at[k, g], cx_r.at[k, g], whole)

    @functools.cache
    def rs_wide(c, g):
        return stage(c, 0, g, True, lambda t: p_sc.at[c, piece(t, g, True)], lambda d: r1.at[c, piece(d, g, True)])

    @functools.cache
    def rs_narrow(c, g):
        n = layout(g)[1]
        return stage(c, 0, g, False, lambda t: q_sc.at[c, g, t, 0:n], lambda d: r2.at[c, g, d, 0:n])

    @functools.cache
    def ag_narrow(c, g):
        return stage(c, 1, g, False, lambda t: own_piece(c, g), lambda d: own_piece(c, g))

    @functools.cache
    def ag_wide(c, g):
        return stage(c, 1, g, True, lambda t: hid.at[c, own_blocks(g)], lambda d: hid.at[c, own_blocks(g)])

    shared = []

    def share(mine, theirs):
        i = len(shared)
        copy = pltpu.make_async_remote_copy(
            mine, mine, co_s.at[i], co_r.at[i], device_id=other, device_id_type=MESH
        )
        copy.start()
        shared.append(
            pltpu.make_async_remote_copy(
                theirs, theirs, co_s.at[i], co_r.at[i], device_id=other, device_id_type=MESH
            )
        )

    seen = []

    def have_shared(upto):
        for copy in shared[len(seen) : upto]:
            copy.wait_recv()
            seen.append(copy)

    def users_of(g):
        first, users, _ = GROUPS[g]
        return slice(first, first + users)

    def blocks_of(g):
        first, users, _ = GROUPS[g]
        return slice(first // 8, (first + users) // 8)

    def batch_users(b):
        return slice(users_of(b[0]).start, users_of(b[-1]).stop)

    def partial_inputs(c, b, visible):
        sums = dot(visible, w_sc[...], 0, 0)
        first = batch_users(b).start // 8
        p_sc[c, first : first + sums.shape[0] // 8] = sums.reshape(sums.shape[0] // 8, 8, F).astype(BF16)
        for g in b:
            start(rs_wide(c, g))

    def first_sum(c, g):
        arrived(rs_wide(c, g))
        n, ring_first = layout(g)[1:]
        for h in range(2 if ring_first else 1):
            for f in range(NZ):
                cut = slice(f * 128, (f + 1) * 128)
                base = layout(g)[0]
                mine = base + (z * 2 * n if ring_first else xy * n) + h * n
                total = p_sc[c, pl.ds(mine, n), :, cut].astype(F32)
                for d in range(1, NZ if ring_first else NXY):
                    slot = base + d * n * (2 if ring_first else 1) + h * n
                    total = total + r1[c, slot : slot + n, :, cut].astype(F32)
                q_sc[c, g, h * NZ + f, 0:n] = total.astype(BF16)
        start(rs_narrow(c, g))

    def second_sum(c, g):
        arrived(rs_narrow(c, g))
        n, ring_first = layout(g)[1:]
        total = q_sc[c, g, xy if ring_first else z, 0:n].astype(F32)
        for d in range(1, NXY if ring_first else NZ):
            total = total + r2[c, g, d, 0:n].astype(F32)
        value = 1.0 / (1.0 + jnp.exp(-(total + hb_ref[own_chunk(g)])))
        own_piece(c, g)[...] = value.astype(BF16)
        start(ag_narrow(c, g))
        return value

    def gather(c, g):
        arrived(ag_narrow(c, g))
        start(ag_wide(c, g))

    def gathered(c, g):
        arrived(ag_wide(c, g))
        rows = hid[c, blocks_of(g)].astype(F32)
        flat[c, core, users_of(g)] = rows.reshape(rows.shape[0] * 8, F).astype(BF16)
        share(flat.at[c, core, users_of(g)], flat.at[c, 1 - core, users_of(g)])

    for b in ((0,), (1,), (2, 3)):
        for u in range(batch_users(b).start // 128, batch_users(b).stop // 128):
            picks = [chosen[u * 16 + k : u * 16 + k + 1] for k in range(CAP)]

            def block(b, carry, picks=picks, u=u):
                base = pl.multiple_of(b * 48, 48)
                at = (lax.broadcasted_iota(jnp.int32, (48, 128), 0) + base).astype(F32)
                hit = picks[0] == at
                for p in picks[1:]:
                    hit = hit | (p == at)
                s_sc[core, pl.ds(base, 48), u * 128 : (u + 1) * 128] = jnp.where(hit, 1.0, 0.0).astype(BF16)
                return carry

            lax.fori_loop(0, COLS // 48, block, 0)
        partial_inputs(0, b, s_sc[core, :, batch_users(b)])
        share(s_sc.at[core, :, batch_users(b)], s_sc.at[1 - core, :, batch_users(b)])
    for step, g in PIPE:
        if step == 0:
            first_sum(0, g)
        elif step == 1:
            pos_own[g, 0 : layout(g)[1]] = second_sum(0, g)
        else:
            gather(0, g)
    for b in BATCHES:
        for g in b:
            gathered(0, g)
        first = batch_users(b).start
        users = batch_users(b).stop - first
        l_sc[:, 0:users] = dot(w_sc[...], flat[0, core, batch_users(b)], 1, 1)

        def softmax(i, carry, first=first, users=users):
            base = pl.multiple_of(i * 16, 16)
            for h in range(users // 128):
                lanes = slice(h * 128, (h + 1) * 128)
                out_lanes = slice(first + h * 128, first + (h + 1) * 128)
                at = [pl.ds(pl.multiple_of(k * PAD + base, 16), 16) for k in range(LEVELS)]
                logits = [l_sc[a, lanes] + vbc[a, :] for a in at]
                largest = functools.reduce(jnp.maximum, logits)
                powers = [jnp.exp(v - largest) for v in logits]
                whole = functools.reduce(jnp.add, powers)
                rated = functools.reduce(jnp.add, [s_sc[core, a, out_lanes].astype(F32) for a in at])
                scale = rated / whole
                for a, v in zip(at, powers):
                    r_sc[core, a, out_lanes] = (v * scale).astype(BF16)
            return carry

        lax.fori_loop(0, PAD // 16, softmax, 0)
        partial_inputs(1, b, r_sc[core, :, batch_users(b)])
        share(r_sc.at[core, :, batch_users(b)], r_sc.at[1 - core, :, batch_users(b)])

    def columns(n):
        return slice(n * 256, (n + 1) * 256)

    for g in SUM_ORDER:
        first_sum(1, g)

    have_shared(len(shared))
    for n in range(F // 256):
        acc_sc[:, columns(n)] = dot(s_sc[0], flat[0, 0, :, columns(n)], 1, 0)
    change = [jnp.zeros((1, 128), F32), jnp.zeros((1, 128), F32)]
    for g in SUM_ORDER:
        value = second_sum(1, g)
        kind = 1 if layout(g)[2] else 0
        moved = jnp.sum(pos_own[g, 0 : layout(g)[1]] - value, axis=0)
        change[kind] = change[kind] + jnp.sum(moved, axis=0, keepdims=True)
    hz[z] = jnp.concatenate(change, axis=0)
    h_z = z_copies(lambda t: hz.at[z], lambda d: hz.at[z], hz_s.at[0], hz_r.at[0], hz.at[0 : NZ - 1])
    start(h_z)
    for n in range(F // 256):
        acc_sc[:, columns(n)] = acc_sc[:, columns(n)] + dot(s_sc[1], flat[0, 1, :, columns(n)], 1, 0)
    for g in SUM_ORDER:
        gather(1, g)
    ones = jnp.ones((8, USERS), BF16)
    for k in range(LEVELS):
        level = slice(k * PAD, (k + 1) * PAD)
        moved = [dot(ones, s_sc[h, level], 1, 1) - dot(ones, r_sc[h, level], 1, 1) for h in range(2)]
        vg_ref[k : k + 1] = (moved[0] + moved[1])[0:1]
    for u in range(4):
        block_rows = hid[0, u * 16 + xy].astype(F32)
        mine = lax.broadcasted_iota(jnp.int32, (8, F), 0) == z
        ph_ref[u : u + 1] = jnp.sum(jnp.where(mine, block_rows, 0.0), axis=0, keepdims=True)

    arrived(h_z)
    rest = functools.reduce(jnp.add, [hz[k, 1:2] for k in range(NZ)])
    for k in range(NZ):
        hxy[xy, k] = hz[k, 0:1] + jnp.where(lax.rem(xy, NZ) == k, rest, 0.0)
    h_xy = xy_copies(
        lambda t: hxy.at[xy], lambda d: hxy.at[xy], hx_s.at[0], hx_r.at[0], hxy.at[0 : NXY - 1]
    )
    start(h_xy)
    upto = []
    for b in BATCHES:
        for g in b:
            gathered(1, g)
        upto.append(len(shared))
    arrived(h_xy)
    total = hxy[0]
    for d in range(1, NXY):
        total = total + hxy[d]
    hco[0] = total
    hg_copy = pltpu.make_async_remote_copy(
        hco.at[0], hco.at[1], hc_s.at[0], hc_r.at[0], device_id=other, device_id_type=MESH
    )
    hg_copy.start()
    for b, last in zip(BATCHES, upto):
        have_shared(last)
        users = batch_users(b)
        for n in range(F // 256):
            moved = dot(r_sc[0, :, users], flat[1, 0, users, columns(n)], 1, 0) + dot(
                r_sc[1, :, users], flat[1, 1, users, columns(n)], 1, 0
            )
            total = acc_sc[:, columns(n)] - moved
            if b != BATCHES[-1]:
                acc_sc[:, columns(n)] = total
                continue
            for k in range(LEVELS):
                wg_ref[k, :, columns(n)] = total[k * PAD : k * PAD + MOV]
    hg_copy.wait_recv()
    for copies in started:
        sent(copies)
    for copy in (hg_copy, *shared):
        copy.wait_send()


def finish(wg_ref, vg_ref, hco_ref, ph_ref, wg_out, vg_out, hg_out, ph_out, vg, hg, sem):
    copies = [
        pltpu.make_async_copy(src, dst, sem.at[i])
        for i, (src, dst) in enumerate(((wg_ref, wg_out), (ph_ref, ph_out), (vg, vg_out), (hg, hg_out)))
    ]
    copies[0].start()
    copies[1].start()
    vg[...] = vg_ref[0:LEVELS, 0:MOV]
    copies[2].start()
    hg[...] = hco_ref[0] + hco_ref[1]
    copies[3].start()
    for copy in copies:
        copy.wait()


def on_device(movie_ids, ratings, valid, weights, vis_bias, hid_bias):
    dma = pltpu.SemaphoreType.DMA
    vmem = pl.BlockSpec(memory_space=pltpu.VMEM)
    hbm = pl.BlockSpec(memory_space=pltpu.HBM)
    shape = jax.ShapeDtypeStruct
    parts = pl.pallas_call(
        kernel,
        out_shape=(
            shape((LEVELS, MOV, F), F32),
            shape((8, PAD), F32),
            shape((2, NZ, 1, 128), F32),
            shape((4, F), F32),
        ),
        in_specs=[hbm] * 6,
        out_specs=(vmem,) * 4,
        scratch_shapes=[
            pltpu.VMEM((4, 128), jnp.int32), pltpu.VMEM((4, 128), jnp.int32), pltpu.VMEM((4, 128), jnp.int32),
            pltpu.VMEM((LEVELS, MOV, F), BF16), pltpu.VMEM((LEVELS, MOV), F32), pltpu.VMEM((NZ, 1, 128), F32),
            dma((6,)),
            pltpu.VMEM((COLS, F), BF16),
            pltpu.VMEM((8, 256), F32),
            pltpu.VMEM((COLS, 128), F32),
            pltpu.VMEM((128, 128), F32),
            pltpu.VMEM((NZ, NXY, 1, 128), F32),
            pltpu.VMEM((NZ, NXY, 1, 128), F32),
            pltpu.VMEM((NXY, NZ, 1, 128), F32),
            pltpu.VMEM((2, COLS, USERS), BF16),
            pltpu.VMEM((2, COLS, USERS), BF16),
            pltpu.VMEM((COLS, WIDEST), F32),
            pltpu.VMEM((2, BLOCKS, 8, F), BF16),
            pltpu.VMEM((2, BLOCKS, 8, F), BF16),
            pltpu.VMEM((2, len(GROUPS), NXY, MOST // 128, 8, 128), BF16),
            pltpu.VMEM((2, len(GROUPS), NXY, MOST // 128, 8, 128), BF16),
            pltpu.VMEM((2, BLOCKS, 8, F), BF16),
            pltpu.VMEM((2, 2, USERS, F), BF16),
            pltpu.VMEM((len(GROUPS), MOST // 128, 8, 128), F32),
            pltpu.VMEM((COLS, F), F32),
            pltpu.VMEM((NZ, 2, 128), F32),
            pltpu.VMEM((NXY, NZ, 1, 128), F32),
            *[dma((1,))] * 4, *[dma((4, len(GROUPS)))] * 4, *[dma((1,))] * 4,
            dma((1,)), dma((1,)), dma((4 * len(GROUPS),)), dma((4 * len(GROUPS),)),
        ],
        compiler_params=pltpu.CompilerParams(
            collective_id=0, has_side_effects=True, vmem_limit_bytes=36 << 20
        ),
    )(*[
        pltpu.with_memory_space_constraint(a, pltpu.HBM)
        for a in (movie_ids, ratings, valid, weights, vis_bias, hid_bias.reshape(NZ, 1, 128))
    ])
    wg, vg, hg, ph = pl.pallas_call(
        finish,
        out_shape=(shape((LEVELS, MOV, F), F32), shape((LEVELS, MOV), F32), shape((NZ, 1, 128), F32), shape((4, F), F32)),
        in_specs=[vmem] * 4,
        out_specs=(hbm,) * 4,
        scratch_shapes=[
            pltpu.VMEM((LEVELS, MOV), F32), pltpu.VMEM((NZ, 1, 128), F32), dma((4,)),
        ],
        compiler_params=pltpu.CompilerParams(vmem_limit_bytes=8 << 20),
    )(*parts)
    return wg, vg, hg.reshape(F), ph


def solution(mesh):
    split = Mesh(mesh.devices.reshape(NZ, 4, 4, mesh.shape["user"]), ALL)
    owner = ("z", "y", "x")
    in_specs = (P(ALL, None), P(ALL, None), P(ALL, None), P(None, owner, None), P(None, owner), P())
    out_specs = (P(None, owner, None), P(None, owner), P(), P(ALL, None))
    return jax.shard_map(on_device, mesh=split, in_specs=in_specs, out_specs=out_specs, check_vma=False)
```
